32 devices in a mesh: sens: 4 (over y, x), par: 8 (over z, core).
Axes of the slice: x: 2, y: 2, z: 4, core: 2. Of those that a mesh axis runs over, the one named last changes fastest.
Arguments:
- kernel: bfloat16 [2, 129, 64, 8192], P(None, None, 'sens', 'par'), may hold values from -0.0625 to 0.0625
- param: float32 [128, 2, 8192], P(None, None, 'par'), may hold values from -6 to 6
- observed: float32 [64, 128], P('sens'), may hold values from -6 to 6
- noise_scale: float32 [64], P('sens'), may hold values from 0.3 to 3
- robust_flags: int32 [64, 128], P('sens'), may hold values 0 or 1
- kappa_field: float32 [8192], P('par'), may hold values from 0.01 to 0.1
- coupling: float32 [8192], P('par'), may hold values from 0.05 to 0.2
- neighbours: int32 [8, 4], replicated, may hold values from -1 to 7, as said below
Outputs:
- gradient: float32 [128, 2, 8192], P(None, None, 'par')
- direction: float32 [128, 2, 8192], P(None, None, 'par')
The draws below stay inside these ranges and needn't reach their ends.
Inputs may be any that keep to these rules, and one draw needn't show every extreme that they name: `neighbours`: row k lists the tiles west, east, south and north of tile k, or -1 where there is none; the tiles fill a grid of 2 columns and 4 rows in an order drawn from the seed, and the relations are mutual.
All inputs are finite; a program needn't handle non-finite values. No bound on the sum of `robust_flags` on one device may be relied on, other than what follows from the above.
Results may differ from the reference program's by a relative error of at most 0.003.
Values may be sent and summed in bfloat16 or wider, within the bound.
A program may use at most 128 MiB of HBM per device.

```python
import math
import jax
import jax.numpy as jnp
from jax import lax

NT = 128
NSAMP = 2
SWEEPS = 8
TSIDE = 32
NF = 129
C_DEV = 1024
NTILES = 8
NC = 8192
NS = 64


def draw_neighbours(key, part):
    tile_count = NTILES
    columns = tile_count // 4
    position = jax.random.permutation(key, tile_count).astype(jnp.int32)
    tile_at = jnp.zeros((tile_count,), jnp.int32).at[position].set(jnp.arange(tile_count, dtype=jnp.int32))
    column_of = position % columns
    row_of = position // columns

    def lookup(inside, target):
        return jnp.where(inside, tile_at[jnp.clip(target, 0, tile_count - 1)], -1)
    west_tile = lookup(column_of > 0, position - 1)
    east_tile = lookup(column_of < columns - 1, position + 1)
    south_tile = lookup(row_of > 0, position - columns)
    north_tile = lookup(row_of < 3, position + columns)
    return jnp.stack([west_tile, east_tile, south_tile, north_tile], 1).astype(jnp.int32)


def place_ends(array, stream_key, smallest, high):
    spot = [jax.random.randint(jax.random.fold_in(stream_key, axis), (), 0, length) for axis, length in enumerate(array.shape)]
    widest = array.shape.index(max(array.shape))
    neighbour = spot[:widest] + [(spot[widest] + 1) % array.shape[widest]] + spot[widest + 1:]
    return array.at[tuple(spot)].set(smallest).at[tuple(neighbour)].set(high)


def block_scale(own_key, dims, pieces, low, top_value):
    level, own = 1.0, jax.random.fold_in(own_key, 6)
    for dim, blocks in pieces:
        steps = jnp.exp(jax.random.uniform(jax.random.fold_in(own, dim), (blocks,), jnp.float32, low / len(pieces), top_value / len(pieces)))
        level = level * jnp.repeat(steps, dims[dim] // blocks).reshape([-1 if axis == dim else 1 for axis in range(len(dims))])
    return level


def noise(rng, extent, width, most, pieces=(), kind=jnp.bfloat16):
    factor_of = block_scale(rng, extent, pieces, -0.22, 0.18) if pieces else 1.0
    drawn = jax.random.normal(rng, extent, jnp.float32) * width * factor_of
    return jnp.minimum(jnp.maximum(drawn, -most), most).astype(kind)


def setup_inputs(seed: int = 0) -> dict:
    arg_keys = jax.random.split(jax.random.key(seed), 9)
    return {
        "kernel": noise(arg_keys[0], (2, NF, NS, NC), NC ** -0.5, 0.0625, ((2, 4), (3, 8))),
        "param": noise(arg_keys[1], (NT, NSAMP, NC), 1.0, 6.0, ((2, 8),), jnp.float32),
        "observed": noise(arg_keys[2], (NS, NT), 1.0, 6.0, ((0, 4),), jnp.float32),
        "noise_scale": jnp.clip(jnp.exp(math.log(3.0) - 2.3025851 * jax.random.uniform(arg_keys[3], (NS,), jnp.float32) ** block_scale(arg_keys[3], (NS,), ((0, 4),), -0.2, 0.2)), 0.3, 3.0),
        "robust_flags": place_ends((jax.random.randint(arg_keys[4], (NS, NT), 0, 2) < 1).astype(jnp.int32), jax.random.fold_in(arg_keys[4], 1), 0, 1),
        "kappa_field": jnp.clip(jnp.exp(math.log(0.1) - 2.3025851 * jax.random.uniform(arg_keys[5], (NC,), jnp.float32) ** block_scale(arg_keys[5], (NC,), ((0, 8),), -0.2, 0.2)), 0.01, 0.1),
        "coupling": jnp.clip(jnp.exp(math.log(0.2) - 1.3862944 * jax.random.uniform(arg_keys[6], (NC,), jnp.float32) ** block_scale(arg_keys[6], (NC,), ((0, 8),), -0.2, 0.2)), 0.05, 0.2),
        "neighbours": draw_neighbours(jax.random.fold_in(arg_keys[8], 71), 0),
    }


huber_limit = 1.345


def tables(length):
    period = 2 * length
    frequency = jnp.arange(length + 1, dtype=jnp.int32)
    moment = jnp.arange(length, dtype=jnp.int32)
    phases = (frequency[:, None] * moment[None, :]) % period
    angles = phases.astype(jnp.float32) * (2.0 * jnp.pi / period)
    cosine = jnp.cos(angles)
    sines = jnp.sin(angles)
    forward = jnp.concatenate([cosine, -sines], 0)
    weight = jnp.where((frequency == 0) | (frequency == length), 1.0, 2.0).astype(jnp.float32) / period
    backward = jnp.concatenate([weight[:, None] * cosine, -weight[:, None] * sines], 0)
    return forward, backward


def residual_spectrum(predicted, observed, noise_scale, robust_flags, backward):
    length = observed.shape[1]
    sensor_count = predicted.shape[1]
    samples = predicted.shape[2]
    series = jnp.dot(backward.T, predicted.reshape(-1, sensor_count * samples), precision=lax.Precision.HIGHEST)
    series = series.reshape(length, sensor_count, samples)
    scaled = (series - observed.T[:, :, None]) / noise_scale[None, :, None]
    robust = jnp.where(robust_flags.T[:, :, None] == 1, jnp.clip(scaled, -huber_limit, huber_limit), scaled)
    weighted = robust / noise_scale[None, :, None]
    spectral = jnp.dot(backward, weighted.reshape(length, -1), precision=lax.Precision.HIGHEST)
    return spectral.reshape(-1, sensor_count, samples)


def neighbour_sum(values, neighbours):
    row_count, tile_count, cell_count = values.shape
    square = values.reshape(row_count, tile_count, TSIDE, TSIDE)
    edge_rows = jnp.stack([square[..., 0], square[..., -1], square[..., 0, :], square[..., -1, :]], 0)

    def facing(edge_index, column_index):
        target = neighbours[:, column_index]
        picked = jnp.take(edge_rows[edge_index], jnp.maximum(target, 0), axis=1)
        return jnp.where((target >= 0)[None, :, None], picked, 0.0)

    west_rim = facing(1, 0)
    east_rim = facing(0, 1)
    south_rim = facing(3, 2)
    north_rim = facing(2, 3)
    column = jnp.arange(cell_count) % TSIDE
    zeros_column = jnp.zeros_like(values[..., :1])
    east_side = jnp.where(column == TSIDE - 1, jnp.repeat(east_rim, TSIDE, axis=-1), jnp.concatenate([values[..., 1:], zeros_column], -1))
    west_side = jnp.where(column == 0, jnp.repeat(west_rim, TSIDE, axis=-1), jnp.concatenate([zeros_column, values[..., :-1]], -1))
    north_side = jnp.concatenate([values[..., TSIDE:], north_rim], -1)
    south_side = jnp.concatenate([south_rim, values[..., :-TSIDE]], -1)
    return east_side + west_side + north_side + south_side


def reference(kernel, param, observed, noise_scale, robust_flags, kappa_field, coupling, neighbours):
    length, samples, cell_total = param.shape
    forward, backward = tables(length)
    spectrum = jnp.dot(forward, param.reshape(length, -1), precision=lax.Precision.HIGHEST)
    spectrum = spectrum.reshape(2, length + 1, samples, cell_total).astype(jnp.bfloat16)

    def predict_one(frequency):
        block = kernel[:, frequency].astype(jnp.float32)
        source = spectrum[:, frequency].astype(jnp.float32)
        product = jnp.einsum('isc,jbc->ijsb', block, source)
        return product[0, 0] - product[1, 1], product[0, 1] + product[1, 0]

    cosine_part, sine_part = lax.map(predict_one, jnp.arange(length + 1))
    predicted = jnp.concatenate([cosine_part, sine_part], 0)
    adjoint = residual_spectrum(predicted, observed, noise_scale, robust_flags, backward).astype(jnp.bfloat16)
    adjoint = adjoint.reshape(2, length + 1, -1, samples)

    def adjoin_one(frequency):
        block = kernel[:, frequency].astype(jnp.float32)
        source = adjoint[:, frequency].astype(jnp.float32)
        product = jnp.einsum('isc,jsb->ijbc', block, source)
        return product[0, 0] + product[1, 1], product[0, 1] - product[1, 0]

    cosine_back, sine_back = lax.map(adjoin_one, jnp.arange(length + 1))
    summed = jnp.concatenate([cosine_back, sine_back], 0).reshape(2 * (length + 1), samples * cell_total)
    misfit = jnp.dot(forward.T, summed, precision=lax.Precision.HIGHEST)
    misfit = misfit.reshape(length * samples, NTILES, C_DEV)
    field_rows = param.reshape(length * samples, NTILES, C_DEV)
    diagonal = (kappa_field + 4.0 * coupling).reshape(NTILES, C_DEV)
    link = coupling.reshape(NTILES, C_DEV)
    gradient = misfit + diagonal * field_rows - link * neighbour_sum(field_rows, neighbours)
    direction = jnp.zeros_like(gradient)
    for sweep in range(SWEEPS):
        direction = (gradient + link * neighbour_sum(direction, neighbours)) / diagonal
    return gradient.reshape(length, samples, cell_total), direction.reshape(length, samples, cell_total)
```

```python
import functools

import jax
import jax.numpy as jnp
from jax import lax
from jax.experimental import pallas as pl
from jax.experimental.pallas import tpu as pltpu
from jax.sharding import PartitionSpec as P

SWEEPS = 8
TSIDE = 32
LANES = 128


huber_limit = 1.345


def tables(length):
    period = 2 * length
    frequency = jnp.arange(length + 1, dtype=jnp.int32)
    moment = jnp.arange(length, dtype=jnp.int32)
    phases = frequency[:, None] * moment[None, :] % period
    angles = phases.astype(jnp.float32) * (2.0 * jnp.pi / period)
    cosine = jnp.cos(angles)
    sines = jnp.sin(angles)
    forward = jnp.concatenate([cosine, -sines], 0)
    weight = (
        jnp.where((frequency == 0) | (frequency == length), 1.0, 2.0).astype(jnp.float32) / period
    )
    backward = jnp.concatenate([weight[:, None] * cosine, -weight[:, None] * sines], 0)
    return (forward, backward)


MESH = pl.DeviceIdType.MESH


def remote(src, dst, send, recv, device):
    return pltpu.make_async_remote_copy(
        src_ref=src, dst_ref=dst, send_sem=send, recv_sem=recv, device_id=device, device_id_type=MESH
    )


def residual_kernel(tiles, series, observed, noise, flags, weighted, landed, send_sem, recv_sem):
    sens, par = lax.axis_index("sens"), lax.axis_index("par")
    barrier = pltpu.get_barrier_semaphore()
    for step in range(1, tiles):
        pl.semaphore_signal(
            barrier, inc=1, device_id=(sens, lax.rem(par + step, tiles)), device_id_type=MESH
        )
    pl.semaphore_wait(barrier, tiles - 1)
    copies = []
    for step in range(1, tiles):
        copy = remote(
            series,
            landed.at[step - 1],
            send_sem.at[step - 1],
            recv_sem.at[step - 1],
            (sens, lax.rem(par + step, tiles)),
        )
        copy.start()
        copies.append(copy)
    total = series[...]
    for step, copy in enumerate(copies):
        copy.wait_recv()
        total = total + landed[step]
    deviation = noise[...][None]
    scaled = (total - observed[...][None]) / deviation
    robust = jnp.where(
        flags[...][None] == 1, jnp.clip(scaled, -huber_limit, huber_limit), scaled
    )
    weighted[...] = robust / deviation
    for copy in copies:
        copy.wait_send()


def residual(series, observed, noise_scale, robust_flags):
    tiles = lax.axis_size("par")
    spread = jnp.broadcast_to(noise_scale[:, None], observed.shape)
    return pl.pallas_call(
        functools.partial(residual_kernel, tiles),
        out_shape=jax.ShapeDtypeStruct(series.shape, jnp.float32),
        in_specs=[pl.BlockSpec(memory_space=pltpu.VMEM)] * 4,
        out_specs=pl.BlockSpec(memory_space=pltpu.VMEM),
        scratch_shapes=[
            pltpu.VMEM((tiles - 1,) + series.shape, jnp.float32),
            pltpu.SemaphoreType.DMA((tiles - 1,)),
            pltpu.SemaphoreType.DMA((tiles - 1,)),
        ],
        compiler_params=pltpu.CompilerParams(collective_id=0, has_side_effects=True),
    )(series, observed, spread, robust_flags)


def grid_sum(load, tile, near, inside, rows, chunks):
    lane = lax.broadcasted_iota(jnp.int32, (rows, LANES), 1)
    column = lax.rem(lane, TSIDE)
    west, east, south, north = (near[tile, side] for side in range(4))
    has_west, has_east, has_south, has_north = (inside[tile, side] for side in range(4))
    own = [load(tile, j) for j in range(chunks)]
    up = [pltpu.roll(v, LANES - TSIDE, 1) for v in own]
    up.append(pltpu.roll(load(north, 0), LANES - TSIDE, 1) * has_north)
    down = [pltpu.roll(load(south, chunks - 1), TSIDE, 1) * has_south]
    down += [pltpu.roll(v, TSIDE, 1) for v in own]
    sums = []
    for j in range(chunks):
        east_rim = pltpu.roll(load(east, j), TSIDE - 1, 1) * has_east
        west_rim = pltpu.roll(load(west, j), LANES - TSIDE + 1, 1) * has_west
        east_side = jnp.where(column == TSIDE - 1, east_rim, pltpu.roll(own[j], LANES - 1, 1))
        west_side = jnp.where(column == 0, west_rim, pltpu.roll(own[j], 1, 1))
        north_side = jnp.where(lane < LANES - TSIDE, up[j], up[j + 1])
        south_side = jnp.where(lane >= TSIDE, down[j + 1], down[j])
        sums.append(east_side + west_side + north_side + south_side)
    return sums


def field_kernel(
    groups, tiles, part, param, coef, near, inside, grad_out, dir_out,
    landed, outgoing, misfit, field, coefs, grad, link, inverse, direction, grad_send, dir_send,
    gathered, a_send, a_recv, p_send, p_recv, c_send, c_recv, b_send, b_recv, g_send, g_recv,
    e_send, e_recv,
):
    sens, par = lax.axis_index("sens"), lax.axis_index("par")
    rows, cells = part.shape[1:]
    chunks = cells // LANES
    group_at = [lax.rem(sens + k, groups) for k in range(groups)]
    tile_at = [lax.rem(par + q, tiles) for q in range(tiles)]
    source_at = [lax.rem(par + tiles - q, tiles) for q in range(tiles)]

    barrier = pltpu.get_barrier_semaphore()
    for k in range(1, groups):
        pl.semaphore_signal(barrier, inc=1, device_id=(group_at[k], par), device_id_type=MESH)
    for q in range(1, tiles):
        pl.semaphore_signal(barrier, inc=1, device_id=(sens, tile_at[q]), device_id_type=MESH)
    pl.semaphore_wait(barrier, groups + tiles - 2)

    order = list(range(1, tiles)) + [0]
    a_copies = {}
    for q in order:
        for k in range(1, groups):
            a_copies[k, q] = remote(
                part.at[group_at[k] * tiles + tile_at[q]],
                landed.at[k - 1, q],
                a_send.at[k - 1, q],
                a_recv.at[k - 1, q],
                (group_at[k], par),
            )
            a_copies[k, q].start()
    p_copies = []
    for q in range(1, tiles):
        device = (sens, tile_at[q])
        p_copies.append(
            remote(coef, coefs.at[par], c_send.at[q - 1], c_recv.at[q - 1], device)
        )
        p_copies.append(
            remote(
                param.at[sens * tiles + tile_at[q]],
                field.at[par],
                p_send.at[q - 1],
                p_recv.at[q - 1],
                device,
            )
        )
    for copy in p_copies:
        copy.start()
    field[par] = param[sens * tiles + par]
    coefs[par] = coef[...]

    b_copies = []
    for q in order:
        total = part[sens * tiles + tile_at[q]].astype(jnp.float32)
        for k in range(1, groups):
            a_copies[k, q].wait_recv()
            total = total + landed[k - 1, q].astype(jnp.float32)
        if q == 0:
            misfit[par] = total.astype(jnp.bfloat16)
        else:
            outgoing[q - 1] = total.astype(jnp.bfloat16)
            copy = remote(
                outgoing.at[q - 1],
                misfit.at[par],
                b_send.at[q - 1],
                b_recv.at[q - 1],
                (sens, tile_at[q]),
            )
            copy.start()
            b_copies.append(copy)
    for copy in p_copies:
        copy.wait_recv()

    def spread(tile, carry):
        both = coefs[tile]
        strength, diagonal = both[0:1], both[1:2]
        link[tile] = jnp.broadcast_to(strength, (rows, cells))
        inverse[tile] = jnp.broadcast_to(1.0 / diagonal, (rows, cells))
        for j, total in enumerate(
            grid_sum(lambda i, j: field[i, :, j * LANES : (j + 1) * LANES], tile, near, inside, rows, chunks)
        ):
            at = slice(j * LANES, (j + 1) * LANES)
            grad[tile, :, at] = diagonal[:, at] * field[tile, :, at] - strength[:, at] * total
        return carry

    lax.fori_loop(0, tiles, spread, 0)
    for copy in b_copies:
        copy.wait_recv()

    def add_misfit(tile, carry):
        total = grad[tile] + misfit[tile].astype(jnp.float32)
        grad[tile] = total
        grad_send[tile] = total.astype(jnp.bfloat16)
        direction[0, tile] = total * inverse[tile]
        return carry

    lax.fori_loop(0, tiles, add_misfit, 0)

    def exchange(which, source):
        copies = []
        for q in range(1, tiles):
            copy = remote(
                source.at[tile_at[q]],
                gathered.at[which, sens, par],
                g_send.at[which, q - 1],
                g_recv.at[which, q - 1],
                (sens, tile_at[q]),
            )
            copy.start()
            copies.append(copy)
        gathered[which, sens, par] = source[par]
        return copies

    def forward_on(which, copies):
        onward = []
        for q in range(tiles):
            if q:
                copies[q - 1].wait_recv()
            piece = gathered.at[which, sens, source_at[q]]
            for k in range(1, groups):
                copy = remote(
                    piece,
                    piece,
                    e_send.at[which, k - 1, q],
                    e_recv.at[which, k - 1, q],
                    (group_at[k], par),
                )
                copy.start()
                onward.append(copy)
        return onward

    def sweep(count, carry):
        old, new = lax.rem(count, 2), lax.rem(count + 1, 2)

        def relax(tile, inner):
            sums = grid_sum(
                lambda i, j: direction[old, i, :, j * LANES : (j + 1) * LANES],
                tile, near, inside, rows, chunks,
            )
            for j, total in enumerate(sums):
                at = slice(j * LANES, (j + 1) * LANES)
                direction[new, tile, :, at] = (
                    grad[tile, :, at] + link[tile, :, at] * total
                ) * inverse[tile, :, at]
            return inner

        return lax.fori_loop(0, tiles, relax, carry)

    g_copies = exchange(0, grad_send)
    lax.fori_loop(0, 3, sweep, 0)
    g_onward = forward_on(0, g_copies)
    lax.fori_loop(3, SWEEPS - 1, sweep, 0)

    def pack(tile, carry):
        dir_send[tile] = direction[(SWEEPS - 1) % 2, tile].astype(jnp.bfloat16)
        return carry

    lax.fori_loop(0, tiles, pack, 0)
    d_copies = exchange(1, dir_send)
    d_onward = forward_on(1, d_copies)

    def unpack(which, out):
        def one(index, carry):
            group, tile = index // tiles, lax.rem(index, tiles)
            out[index] = gathered[which, group, tile].astype(jnp.float32)
            return carry

        lax.fori_loop(0, groups * tiles, one, 0)

    for copy in g_onward:
        copy.wait_recv()
    unpack(0, grad_out)
    for copy in d_onward:
        copy.wait_recv()
    unpack(1, dir_out)
    for copy in list(a_copies.values()) + p_copies + b_copies + g_copies + d_copies + g_onward + d_onward:
        copy.wait_send()


def field_stage(part, param, coef, neighbours):
    groups, tiles = lax.axis_size("sens"), lax.axis_size("par")
    rows, cells = part.shape[1:]
    f32, bf16 = jnp.float32, jnp.bfloat16
    near = jnp.maximum(neighbours, 0)
    inside = (neighbours >= 0).astype(f32)
    full = jax.ShapeDtypeStruct(param.shape, f32)
    dma = pltpu.SemaphoreType.DMA
    block = (tiles, rows, cells)
    vmem, smem = pl.BlockSpec(memory_space=pltpu.VMEM), pl.BlockSpec(memory_space=pltpu.SMEM)
    sems = [(groups - 1, tiles), (tiles - 1,), (tiles - 1,), (tiles - 1,), (2, tiles - 1), (2, groups - 1, tiles)]
    return pl.pallas_call(
        functools.partial(field_kernel, groups, tiles),
        out_shape=(full, full),
        in_specs=[vmem, vmem, vmem, smem, smem],
        out_specs=(vmem, vmem),
        scratch_shapes=[
            pltpu.VMEM((groups - 1,) + block, bf16),
            pltpu.VMEM((tiles - 1, rows, cells), bf16),
            pltpu.VMEM(block, bf16),
            pltpu.VMEM(block, f32),
            pltpu.VMEM((tiles, 2, cells), f32),
            pltpu.VMEM(block, f32),
            pltpu.VMEM(block, f32),
            pltpu.VMEM(block, f32),
            pltpu.VMEM((2,) + block, f32),
            pltpu.VMEM(block, bf16),
            pltpu.VMEM(block, bf16),
            pltpu.VMEM((2, groups) + block, bf16),
        ]
        + [dma(shape) for shape in sems for _ in range(2)],
        compiler_params=pltpu.CompilerParams(collective_id=1, has_side_effects=True),
    )(part, param, coef, near, inside)


def per_device(
    kernel, param, observed, noise_scale, robust_flags, kappa_field, coupling, neighbours
):
    length, samples, cell_count = param.shape
    sensor_count = observed.shape[0]
    spectra_rows = 2 * (length + 1)
    forward, backward = tables(length)
    spectrum = jnp.dot(forward, param.reshape(length, -1), precision=lax.Precision.HIGHEST)
    spectrum = spectrum.reshape(2, length + 1, samples, cell_count).astype(jnp.bfloat16)
    product = jnp.einsum("ifsc,jfbc->ijfsb", kernel, spectrum, preferred_element_type=jnp.float32)
    partial_sum = jnp.concatenate([product[0, 0] - product[1, 1], product[0, 1] + product[1, 0]], 0)
    series = jnp.einsum("ft,fsb->bst", backward, partial_sum, precision=lax.Precision.HIGHEST)
    weighted = residual(series, observed, noise_scale, robust_flags)
    adjoint = jnp.einsum("ft,bst->fsb", backward, weighted, precision=lax.Precision.HIGHEST)
    adjoint = adjoint.astype(jnp.bfloat16).reshape(2, length + 1, sensor_count, samples)
    back_product = jnp.einsum(
        "ifsc,jfsb->ijfbc", kernel, adjoint, preferred_element_type=jnp.float32
    )
    partial_grad = jnp.concatenate(
        [back_product[0, 0] + back_product[1, 1], back_product[0, 1] - back_product[1, 0]], 0
    )
    partial_grad = partial_grad.reshape(spectra_rows, samples * cell_count)
    misfit = jnp.dot(forward.T, partial_grad, precision=lax.Precision.HIGHEST)
    devices = lax.axis_size("sens") * lax.axis_size("par")
    blocks = (devices, length * samples // devices, cell_count)
    coef = jnp.stack([coupling, kappa_field + 4.0 * coupling], 0)
    gradient, direction = field_stage(
        misfit.astype(jnp.bfloat16).reshape(blocks), param.reshape(blocks), coef, neighbours
    )
    return gradient.reshape(param.shape), direction.reshape(param.shape)


def solution(mesh):
    return jax.shard_map(
        per_device,
        mesh=mesh,
        in_specs=(
            P(None, None, "sens", "par"),
            P(None, None, "par"),
            P("sens", None),
            P("sens"),
            P("sens", None),
            P("par"),
            P("par"),
            P(),
        ),
        out_specs=(P(None, None, "par"), P(None, None, "par")),
        check_vma=False,
    )
```

```python
import functools

import jax
import jax.numpy as jnp
from jax import lax
from jax.experimental import pallas as pl
from jax.experimental.pallas import tpu as pltpu
from jax.sharding import PartitionSpec as P

SWEEPS = 8
TSIDE = 32
LANES = 128


huber_limit = 1.345


def tables(length):
    period = 2 * length
    frequency = jnp.arange(length + 1, dtype=jnp.int32)
    moment = jnp.arange(length, dtype=jnp.int32)
    phases = frequency[:, None] * moment[None, :] % period
    angles = phases.astype(jnp.float32) * (2.0 * jnp.pi / period)
    cosine = jnp.cos(angles)
    sines = jnp.sin(angles)
    forward = jnp.concatenate([cosine, -sines], 0)
    weight = (
        jnp.where((frequency == 0) | (frequency == length), 1.0, 2.0).astype(jnp.float32) / period
    )
    backward = jnp.concatenate([weight[:, None] * cosine, -weight[:, None] * sines], 0)
    return (forward, backward)


MESH = pl.DeviceIdType.MESH


def remote(src, dst, send, recv, device):
    return pltpu.make_async_remote_copy(
        src_ref=src, dst_ref=dst, send_sem=send, recv_sem=recv, device_id=device, device_id_type=MESH
    )


def residual_kernel(tiles, series, observed, noise, flags, weighted, landed, send_sem, recv_sem):
    sens, par = lax.axis_index("sens"), lax.axis_index("par")
    barrier = pltpu.get_barrier_semaphore()
    for step in range(1, tiles):
        pl.semaphore_signal(
            barrier, inc=1, device_id=(sens, lax.rem(par + step, tiles)), device_id_type=MESH
        )
    pl.semaphore_wait(barrier, tiles - 1)
    copies = []
    for step in range(1, tiles):
        copy = remote(
            series,
            landed.at[step - 1],
            send_sem.at[step - 1],
            recv_sem.at[step - 1],
            (sens, lax.rem(par + step, tiles)),
        )
        copy.start()
        copies.append(copy)
    total = series[...]
    for step, copy in enumerate(copies):
        copy.wait_recv()
        total = total + landed[step]
    deviation = noise[...]
    scaled = (total - observed[...]) / deviation
    robust = jnp.where(
        flags[...] == 1, jnp.clip(scaled, -huber_limit, huber_limit), scaled
    )
    weighted[...] = robust / deviation
    for copy in copies:
        copy.wait_send()


def residual(series, observed, noise_scale, robust_flags):
    tiles = lax.axis_size("par")
    spread = jnp.broadcast_to(noise_scale[:, None], observed.shape)
    return pl.pallas_call(
        functools.partial(residual_kernel, tiles),
        out_shape=jax.ShapeDtypeStruct(series.shape, jnp.float32),
        in_specs=[pl.BlockSpec(memory_space=pltpu.VMEM)] * 4,
        out_specs=pl.BlockSpec(memory_space=pltpu.VMEM),
        scratch_shapes=[
            pltpu.VMEM((tiles - 1,) + series.shape, jnp.float32),
            pltpu.SemaphoreType.DMA((tiles - 1,)),
            pltpu.SemaphoreType.DMA((tiles - 1,)),
        ],
        compiler_params=pltpu.CompilerParams(collective_id=0, has_side_effects=True),
    )(series, observed, spread, robust_flags)


def grid_sum(load, tile, near, rows, chunks):
    lane = lax.broadcasted_iota(jnp.int32, (rows, LANES), 1)
    column = lax.rem(lane, TSIDE)
    beside = [near[tile, side] for side in range(4)]
    west, east, south, north = (jnp.maximum(index, 0) for index in beside)
    has_west, has_east, has_south, has_north = (
        jnp.minimum(index + 1, 1).astype(jnp.float32) for index in beside
    )
    own = [load(tile, j) for j in range(chunks)]
    up = [pltpu.roll(v, LANES - TSIDE, 1) for v in own]
    up.append(pltpu.roll(load(north, 0), LANES - TSIDE, 1) * has_north)
    down = [pltpu.roll(load(south, chunks - 1), TSIDE, 1) * has_south]
    down += [pltpu.roll(v, TSIDE, 1) for v in own]
    sums = []
    for j in range(chunks):
        east_rim = pltpu.roll(load(east, j), TSIDE - 1, 1) * has_east
        west_rim = pltpu.roll(load(west, j), LANES - TSIDE + 1, 1) * has_west
        east_side = jnp.where(column == TSIDE - 1, east_rim, pltpu.roll(own[j], LANES - 1, 1))
        west_side = jnp.where(column == 0, west_rim, pltpu.roll(own[j], 1, 1))
        north_side = jnp.where(lane < LANES - TSIDE, up[j], up[j + 1])
        south_side = jnp.where(lane >= TSIDE, down[j + 1], down[j])
        sums.append(east_side + west_side + north_side + south_side)
    return sums


def field_kernel(
    groups, tiles, part, param, coef, near, grad_out, dir_out,
    landed, outgoing, misfit, field, coefs, grad, link, inverse, direction, grad_send, dir_send,
    gathered, a_send, a_recv, p_send, p_recv, c_send, c_recv, b_send, b_recv, g_send, g_recv,
    e_send, e_recv,
):
    sens, par = lax.axis_index("sens"), lax.axis_index("par")
    rows, cells = part.shape[1:]
    chunks = cells // LANES
    group_at = [lax.rem(sens + k, groups) for k in range(groups)]
    tile_at = [lax.rem(par + q, tiles) for q in range(tiles)]
    source_at = [lax.rem(par + tiles - q, tiles) for q in range(tiles)]

    barrier = pltpu.get_barrier_semaphore()
    for k in range(1, groups):
        pl.semaphore_signal(barrier, inc=1, device_id=(group_at[k], par), device_id_type=MESH)
    for q in range(1, tiles):
        pl.semaphore_signal(barrier, inc=1, device_id=(sens, tile_at[q]), device_id_type=MESH)
    pl.semaphore_wait(barrier, groups + tiles - 2)

    order = list(range(1, tiles)) + [0]
    a_copies = {}
    for q in order:
        for k in range(1, groups):
            a_copies[k, q] = remote(
                part.at[group_at[k] * tiles + tile_at[q]],
                landed.at[k - 1, q],
                a_send.at[k - 1, q],
                a_recv.at[k - 1, q],
                (group_at[k], par),
            )
            a_copies[k, q].start()
    p_copies = []
    for q in range(1, tiles):
        device = (sens, tile_at[q])
        p_copies.append(
            remote(coef, coefs.at[par], c_send.at[q - 1], c_recv.at[q - 1], device)
        )
        p_copies.append(
            remote(
                param.at[sens * tiles + tile_at[q]],
                field.at[par],
                p_send.at[q - 1],
                p_recv.at[q - 1],
                device,
            )
        )
    for copy in p_copies:
        copy.start()
    field[par] = param[sens * tiles + par]
    coefs[par] = coef[...]

    b_copies = []
    for q in order:
        total = part[sens * tiles + tile_at[q]].astype(jnp.float32)
        for k in range(1, groups):
            a_copies[k, q].wait_recv()
            total = total + landed[k - 1, q].astype(jnp.float32)
        if q == 0:
            misfit[par] = total
        else:
            outgoing[q - 1] = total
            copy = remote(
                outgoing.at[q - 1],
                misfit.at[par],
                b_send.at[q - 1],
                b_recv.at[q - 1],
                (sens, tile_at[q]),
            )
            copy.start()
            b_copies.append(copy)
    for copy in p_copies:
        copy.wait_recv()

    def spread(tile, carry):
        both = coefs[tile]
        strength, diagonal = both[0:1], both[1:2]
        link[tile] = jnp.broadcast_to(strength, (rows, cells))
        inverse[tile] = jnp.broadcast_to(1.0 / diagonal, (rows, cells))
        for j, total in enumerate(
            grid_sum(lambda i, j: field[i, :, j * LANES : (j + 1) * LANES], tile, near, rows, chunks)
        ):
            at = slice(j * LANES, (j + 1) * LANES)
            grad[tile, :, at] = diagonal[:, at] * field[tile, :, at] - strength[:, at] * total
        return carry

    lax.fori_loop(0, tiles, spread, 0)
    for copy in b_copies:
        copy.wait_recv()

    def add_misfit(tile, carry):
        total = grad[tile] + misfit[tile]
        grad[tile] = total
        grad_send[tile] = total.astype(jnp.bfloat16)
        direction[0, tile] = total * inverse[tile]
        return carry

    lax.fori_loop(0, tiles, add_misfit, 0)

    def exchange(which, source):
        copies = []
        for q in range(1, tiles):
            copy = remote(
                source.at[tile_at[q]],
                gathered.at[which, sens, par],
                g_send.at[which, q - 1],
                g_recv.at[which, q - 1],
                (sens, tile_at[q]),
            )
            copy.start()
            copies.append(copy)
        gathered[which, sens, par] = source[par]
        return copies

    def forward_on(which, copies):
        onward = []
        for q in range(tiles):
            if q:
                copies[q - 1].wait_recv()
            piece = gathered.at[which, sens, source_at[q]]
            for k in range(1, groups):
                copy = remote(
                    piece,
                    piece,
                    e_send.at[which, k - 1, q],
                    e_recv.at[which, k - 1, q],
                    (group_at[k], par),
                )
                copy.start()
                onward.append(copy)
        return onward

    def sweep(count, carry):
        old, new = lax.rem(count, 2), lax.rem(count + 1, 2)

        def relax(tile, inner):
            sums = grid_sum(
                lambda i, j: direction[old, i, :, j * LANES : (j + 1) * LANES],
                tile, near, rows, chunks,
            )
            for j, total in enumerate(sums):
                at = slice(j * LANES, (j + 1) * LANES)
                direction[new, tile, :, at] = (
                    grad[tile, :, at] + link[tile, :, at] * total
                ) * inverse[tile, :, at]
            return inner

        return lax.fori_loop(0, tiles, relax, carry)

    g_copies = exchange(0, grad_send)
    lax.fori_loop(0, 3, sweep, 0)
    g_onward = forward_on(0, g_copies)
    lax.fori_loop(3, SWEEPS - 1, sweep, 0)

    def pack(tile, carry):
        dir_send[tile] = direction[(SWEEPS - 1) % 2, tile].astype(jnp.bfloat16)
        return carry

    lax.fori_loop(0, tiles, pack, 0)
    d_copies = exchange(1, dir_send)
    d_onward = forward_on(1, d_copies)

    def unpack(which, out):
        def one(index, carry):
            group, tile = index // tiles, lax.rem(index, tiles)
            out[index] = gathered[which, group, tile].astype(jnp.float32)
            return carry

        lax.fori_loop(0, groups * tiles, one, 0)

    for copy in g_onward:
        copy.wait_recv()
    unpack(0, grad_out)
    for copy in d_onward:
        copy.wait_recv()
    unpack(1, dir_out)
    for copy in list(a_copies.values()) + p_copies + b_copies + g_copies + d_copies + g_onward + d_onward:
        copy.wait_send()


def field_stage(part, param, coef, neighbours):
    groups, tiles = lax.axis_size("sens"), lax.axis_size("par")
    rows, cells = part.shape[1:]
    f32, bf16 = jnp.float32, jnp.bfloat16
    full = jax.ShapeDtypeStruct(param.shape, f32)
    dma = pltpu.SemaphoreType.DMA
    block = (tiles, rows, cells)
    vmem, smem = pl.BlockSpec(memory_space=pltpu.VMEM), pl.BlockSpec(memory_space=pltpu.SMEM)
    sems = [(groups - 1, tiles), (tiles - 1,), (tiles - 1,), (tiles - 1,), (2, tiles - 1), (2, groups - 1, tiles)]
    return pl.pallas_call(
        functools.partial(field_kernel, groups, tiles),
        out_shape=(full, full),
        in_specs=[vmem, vmem, vmem, smem],
        out_specs=(vmem, vmem),
        scratch_shapes=[
            pltpu.VMEM((groups - 1,) + block, bf16),
            pltpu.VMEM((tiles - 1, rows, cells), f32),
            pltpu.VMEM(block, f32),
            pltpu.VMEM(block, f32),
            pltpu.VMEM((tiles, 2, cells), f32),
            pltpu.VMEM(block, f32),
            pltpu.VMEM(block, f32),
            pltpu.VMEM(block, f32),
            pltpu.VMEM((2,) + block, f32),
            pltpu.VMEM(block, bf16),
            pltpu.VMEM(block, bf16),
            pltpu.VMEM((2, groups) + block, bf16),
        ]
        + [dma(shape) for shape in sems for _ in range(2)],
        compiler_params=pltpu.CompilerParams(collective_id=1, has_side_effects=True),
    )(part, param, coef, neighbours)


HIGH = lax.Precision.HIGHEST
LAST = (((1,), (1,)), ((), ()))


def block_tables(length, samples):
    forward, backward = tables(length)
    count = length + 1
    size = max(d for d in range(1, 65) if count % d == 0)
    padded = -(-size // 4) * 4
    blocks = count // size
    eye = jnp.eye(samples, dtype=jnp.float32)

    def arrange(table):
        table = table.reshape(2, blocks, size, length)
        return jnp.pad(table, ((0, 0), (0, 0), (0, padded - size), (0, 0)))

    fore, back = arrange(forward), arrange(backward)
    turned = jnp.stack([back[1], -back[0]], 0)
    rows = samples * 2 * padded
    fields = jnp.einsum("jkft,bd->kbjftd", fore, eye).reshape(blocks, rows, -1)
    sensors = [
        jnp.einsum("jkft,bd->kbjfdt", table, eye).reshape(blocks, rows, -1)
        for table in (back, turned)
    ]
    return fields, jnp.stack(sensors, 1), size, padded


def diagonal(shape, width, padded, frequency_dim):
    own = lax.broadcasted_iota(jnp.int32, shape, frequency_dim)
    other = lax.broadcasted_iota(jnp.int32, shape, 1 - frequency_dim)
    return own // width == lax.rem(other, padded)


def predict_kernel(padded, kernel, param, fields, sensors, series):
    size, sensor_count, cells = kernel.shape[1:]
    spectrum = jnp.dot(fields[0], param[...], precision=HIGH, preferred_element_type=jnp.float32)
    spectrum = spectrum.astype(jnp.bfloat16)
    total = jnp.zeros(series.shape, jnp.float32)
    for i in range(2):
        product = lax.dot_general(
            kernel[i].reshape(size * sensor_count, cells),
            spectrum,
            LAST,
            preferred_element_type=jnp.float32,
        )
        product = jnp.where(diagonal(product.shape, sensor_count, padded, 0), product, 0.0)
        timed = jnp.dot(product, sensors[0, i], precision=HIGH, preferred_element_type=jnp.float32)
        total = total + jnp.sum(timed.reshape(size, sensor_count, -1), 0)

    @pl.when(pl.program_id(0) == 0)
    def _():
        series[...] = jnp.zeros_like(series)

    series[...] += total


def predict(kernel, param, fields, sensors, size, padded):
    blocks, rows, width = fields.shape
    sensor_count, cells = kernel.shape[2:]
    return pl.pallas_call(
        functools.partial(predict_kernel, padded),
        out_shape=jax.ShapeDtypeStruct((sensor_count, width), jnp.float32),
        grid=(blocks,),
        in_specs=[
            pl.BlockSpec((2, size, sensor_count, cells), lambda k: (0, k, 0, 0)),
            pl.BlockSpec(param.shape, lambda k: (0, 0)),
            pl.BlockSpec((1, rows, width), lambda k: (k, 0, 0)),
            pl.BlockSpec((1, 2, rows, width), lambda k: (k, 0, 0, 0)),
        ],
        out_specs=pl.BlockSpec((sensor_count, width), lambda k: (0, 0)),
    )(kernel, param, fields, sensors)


def backward_kernel(padded, blocks, kernel, weighted, fields, sensors, part, total):
    size, sensor_count, cells = kernel.shape[1:]
    rows = sensors.shape[2]
    pairs = size * sensor_count
    copies = lax.rem(lax.broadcasted_iota(jnp.int32, (sensor_count, pairs), 1), sensor_count)
    copies = copies == lax.broadcasted_iota(jnp.int32, (sensor_count, pairs), 0)
    copies = jnp.where(copies, 1.0, 0.0).astype(jnp.bfloat16)
    keep = diagonal((rows, pairs), sensor_count, padded, 1)
    back = jnp.zeros((rows, cells), jnp.float32)
    for i in range(2):
        adjoint = lax.dot_general(
            sensors[0, i], weighted[...], LAST, precision=HIGH, preferred_element_type=jnp.float32
        )
        wide = jnp.dot(adjoint.astype(jnp.bfloat16), copies, preferred_element_type=jnp.float32)
        wide = jnp.where(keep, wide, 0.0).astype(jnp.bfloat16)
        back = back + jnp.dot(
            wide, kernel[i].reshape(pairs, cells), preferred_element_type=jnp.float32
        )
    misfit = jnp.dot(fields[0], back, precision=HIGH, preferred_element_type=jnp.float32)

    @pl.when(pl.program_id(0) == 0)
    def _():
        total[...] = jnp.zeros_like(total)

    total[...] += misfit

    @pl.when(pl.program_id(0) == blocks - 1)
    def _():
        part[...] = total[...].reshape(part.shape).astype(part.dtype)


def back_project(kernel, weighted, fields, sensors, size, padded, shape):
    blocks, width, rows = fields.shape
    sensor_count, cells = kernel.shape[2:]
    return pl.pallas_call(
        functools.partial(backward_kernel, padded, blocks),
        out_shape=jax.ShapeDtypeStruct(shape, jnp.bfloat16),
        grid=(blocks,),
        in_specs=[
            pl.BlockSpec((2, size, sensor_count, cells), lambda k: (0, k, 0, 0)),
            pl.BlockSpec(weighted.shape, lambda k: (0, 0)),
            pl.BlockSpec((1, width, rows), lambda k: (k, 0, 0)),
            pl.BlockSpec((1, 2, rows, weighted.shape[1]), lambda k: (k, 0, 0, 0)),
        ],
        out_specs=pl.BlockSpec(shape, lambda k: (0, 0, 0)),
        scratch_shapes=[pltpu.VMEM((width, cells), jnp.float32)],
    )(kernel, weighted, fields, sensors)


def per_device(
    kernel, param, observed, noise_scale, robust_flags, kappa_field, coupling, neighbours
):
    length, samples, cell_count = param.shape
    fields, sensors, size, padded = block_tables(length, samples)
    devices = lax.axis_size("sens") * lax.axis_size("par")
    blocks = (devices, length * samples // devices, cell_count)
    flat = param.reshape(length * samples, cell_count)
    series = predict(kernel, flat, fields, sensors, size, padded)
    weighted = residual(
        series,
        jnp.tile(observed, (1, samples)),
        noise_scale,
        jnp.tile(robust_flags, (1, samples)),
    )
    part = back_project(
        kernel, weighted, fields.transpose(0, 2, 1), sensors, size, padded, blocks
    )
    coef = jnp.stack([coupling, kappa_field + 4.0 * coupling], 0)
    gradient, direction = field_stage(part, flat.reshape(blocks), coef, neighbours)
    return gradient.reshape(param.shape), direction.reshape(param.shape)


def solution(mesh):
    return jax.shard_map(
        per_device,
        mesh=mesh,
        in_specs=(
            P(None, None, "sens", "par"),
            P(None, None, "par"),
            P("sens", None),
            P("sens"),
            P("sens", None),
            P("par"),
            P("par"),
            P(),
        ),
        out_specs=(P(None, None, "par"), P(None, None, "par")),
        check_vma=False,
    )
```

```python
import functools

import jax
import jax.numpy as jnp
import numpy as np
from jax import lax
from jax.experimental import pallas as pl
from jax.experimental.pallas import tpu as pltpu
from jax.sharding import PartitionSpec as P

SWEEPS = 8
TSIDE = 32
LANES = 128


huber_limit = 1.345


def tables(length):
    period = 2 * length
    frequency = np.arange(length + 1)
    phases = frequency[:, None] * np.arange(length)[None, :] % period
    angles = phases * (2.0 * np.pi / period)
    cosine, sines = np.cos(angles), np.sin(angles)
    forward = np.stack([cosine, -sines], 0)
    weight = np.where((frequency == 0) | (frequency == length), 1.0, 2.0) / period
    return forward, forward * weight[:, None]


MESH = pl.DeviceIdType.MESH


def remote(src, dst, send, recv, device):
    return pltpu.make_async_remote_copy(
        src_ref=src, dst_ref=dst, send_sem=send, recv_sem=recv, device_id=device, device_id_type=MESH
    )


def residual_kernel(tiles, series, observed, noise, flags, weighted, landed, send_sem, recv_sem):
    sens, par = lax.axis_index("sens"), lax.axis_index("par")
    barrier = pltpu.get_barrier_semaphore()
    for step in range(1, tiles):
        pl.semaphore_signal(
            barrier, inc=1, device_id=(sens, lax.rem(par + step, tiles)), device_id_type=MESH
        )
    pl.semaphore_wait(barrier, tiles - 1)
    copies = []
    for step in range(1, tiles):
        copy = remote(
            series,
            landed.at[step - 1],
            send_sem.at[step - 1],
            recv_sem.at[step - 1],
            (sens, lax.rem(par + step, tiles)),
        )
        copy.start()
        copies.append(copy)
    total = series[...]
    for step, copy in enumerate(copies):
        copy.wait_recv()
        total = total + landed[step]
    samples = series.shape[1] // observed.shape[1]

    def widen(ref):
        return jnp.concatenate([ref[...]] * samples, 1)

    deviation = widen(noise)
    scaled = (total - widen(observed)) / deviation
    robust = jnp.where(
        widen(flags) == 1, jnp.clip(scaled, -huber_limit, huber_limit), scaled
    )
    weighted[...] = robust / deviation
    for copy in copies:
        copy.wait_send()


def residual(series, observed, noise_scale, robust_flags):
    tiles = lax.axis_size("par")
    spread = jnp.broadcast_to(noise_scale[:, None], observed.shape)
    return pl.pallas_call(
        functools.partial(residual_kernel, tiles),
        out_shape=jax.ShapeDtypeStruct(series.shape, jnp.float32),
        in_specs=[pl.BlockSpec(memory_space=pltpu.VMEM)] * 4,
        out_specs=pl.BlockSpec(memory_space=pltpu.VMEM),
        scratch_shapes=[
            pltpu.VMEM((tiles - 1,) + series.shape, jnp.float32),
            pltpu.SemaphoreType.DMA((tiles - 1,)),
            pltpu.SemaphoreType.DMA((tiles - 1,)),
        ],
        compiler_params=pltpu.CompilerParams(collective_id=0, has_side_effects=True),
    )(series, observed, spread, robust_flags)


def grid_sum(load, tile, near, rows, chunks):
    lane = lax.broadcasted_iota(jnp.int32, (rows, LANES), 1)
    column = lax.rem(lane, TSIDE)
    beside = [near[tile, side] for side in range(4)]
    west, east, south, north = (jnp.maximum(index, 0) for index in beside)
    has_west, has_east, has_south, has_north = (
        jnp.minimum(index + 1, 1).astype(jnp.float32) for index in beside
    )
    own = [load(tile, j) for j in range(chunks)]
    up = [pltpu.roll(v, LANES - TSIDE, 1) for v in own]
    up.append(pltpu.roll(load(north, 0), LANES - TSIDE, 1) * has_north)
    down = [pltpu.roll(load(south, chunks - 1), TSIDE, 1) * has_south]
    down += [pltpu.roll(v, TSIDE, 1) for v in own]
    sums = []
    for j in range(chunks):
        east_rim = pltpu.roll(load(east, j), TSIDE - 1, 1) * has_east
        west_rim = pltpu.roll(load(west, j), LANES - TSIDE + 1, 1) * has_west
        east_side = jnp.where(column == TSIDE - 1, east_rim, pltpu.roll(own[j], LANES - 1, 1))
        west_side = jnp.where(column == 0, west_rim, pltpu.roll(own[j], 1, 1))
        north_side = jnp.where(lane < LANES - TSIDE, up[j], up[j + 1])
        south_side = jnp.where(lane >= TSIDE, down[j + 1], down[j])
        sums.append(east_side + west_side + north_side + south_side)
    return sums


def field_kernel(
    groups, tiles, part, param, coef, near, grad_out, dir_out,
    landed, outgoing, misfit, field, coefs, grad, link, inverse, even, odd, grad_send, dir_send,
    gathered, a_send, a_recv, p_send, p_recv, c_send, c_recv, b_send, b_recv, g_send, g_recv,
    e_send, e_recv,
):
    sens, par = lax.axis_index("sens"), lax.axis_index("par")
    rows, cells = part.shape[1:]
    chunks = cells // LANES
    group_at = [lax.rem(sens + k, groups) for k in range(groups)]
    tile_at = [lax.rem(par + q, tiles) for q in range(tiles)]
    source_at = [lax.rem(par + tiles - q, tiles) for q in range(tiles)]

    barrier = pltpu.get_barrier_semaphore()
    for k in range(1, groups):
        pl.semaphore_signal(barrier, inc=1, device_id=(group_at[k], par), device_id_type=MESH)
    for q in range(1, tiles):
        pl.semaphore_signal(barrier, inc=1, device_id=(sens, tile_at[q]), device_id_type=MESH)
    pl.semaphore_wait(barrier, groups + tiles - 2)

    order = list(range(1, tiles)) + [0]
    a_copies = {}
    for q in order:
        for k in range(1, groups):
            a_copies[k, q] = remote(
                part.at[group_at[k] * tiles + tile_at[q]],
                landed.at[k - 1, q],
                a_send.at[k - 1, q],
                a_recv.at[k - 1, q],
                (group_at[k], par),
            )
            a_copies[k, q].start()
    p_copies = []
    for q in range(1, tiles):
        device = (sens, tile_at[q])
        p_copies.append(
            remote(coef, coefs.at[par], c_send.at[q - 1], c_recv.at[q - 1], device)
        )
        p_copies.append(
            remote(
                param.at[sens * tiles + tile_at[q]],
                field.at[par],
                p_send.at[q - 1],
                p_recv.at[q - 1],
                device,
            )
        )
    for copy in p_copies:
        copy.start()
    field[par] = param[sens * tiles + par]
    coefs[par] = coef[...]

    b_copies = []
    for q in order:
        total = part[sens * tiles + tile_at[q]].astype(jnp.float32)
        for k in range(1, groups):
            a_copies[k, q].wait_recv()
            total = total + landed[k - 1, q].astype(jnp.float32)
        if q == 0:
            misfit[par] = total
        else:
            outgoing[q - 1] = total
            copy = remote(
                outgoing.at[q - 1],
                misfit.at[par],
                b_send.at[q - 1],
                b_recv.at[q - 1],
                (sens, tile_at[q]),
            )
            copy.start()
            b_copies.append(copy)
    for copy in p_copies:
        copy.wait_recv()

    def spread(tile, carry):
        both = coefs[tile]
        strength, diagonal = both[0:1], both[1:2]
        link[tile] = jnp.broadcast_to(strength, (rows, cells))
        inverse[tile] = jnp.broadcast_to(1.0 / diagonal, (rows, cells))
        for j, total in enumerate(
            grid_sum(lambda i, j: field[i, :, j * LANES : (j + 1) * LANES], tile, near, rows, chunks)
        ):
            at = slice(j * LANES, (j + 1) * LANES)
            grad[tile, :, at] = diagonal[:, at] * field[tile, :, at] - strength[:, at] * total
        return carry

    lax.fori_loop(0, tiles, spread, 0)
    for copy in b_copies:
        copy.wait_recv()

    def add_misfit(tile, carry):
        total = grad[tile] + misfit[tile]
        grad[tile] = total
        grad_send[tile] = total.astype(jnp.bfloat16)
        even[tile] = total * inverse[tile]
        return carry

    lax.fori_loop(0, tiles, add_misfit, 0)

    def exchange(which, source):
        copies = []
        for q in range(1, tiles):
            copy = remote(
                source.at[tile_at[q]],
                gathered.at[which, sens, par],
                g_send.at[which, q - 1],
                g_recv.at[which, q - 1],
                (sens, tile_at[q]),
            )
            copy.start()
            copies.append(copy)
        gathered[which, sens, par] = source[par]
        return copies

    def forward_on(which, copies):
        onward = []
        for q in range(tiles):
            if q:
                copies[q - 1].wait_recv()
            piece = gathered.at[which, sens, source_at[q]]
            for k in range(1, groups):
                copy = remote(
                    piece,
                    piece,
                    e_send.at[which, k - 1, q],
                    e_recv.at[which, k - 1, q],
                    (group_at[k], par),
                )
                copy.start()
                onward.append(copy)
        return onward

    def sweep(count):
        old, new = (even, odd) if count % 2 == 0 else (odd, even)

        def relax(tile, carry):
            sums = grid_sum(
                lambda i, j: old[i, :, j * LANES : (j + 1) * LANES], tile, near, rows, chunks
            )
            for j, total in enumerate(sums):
                at = slice(j * LANES, (j + 1) * LANES)
                new[tile, :, at] = (grad[tile, :, at] + link[tile, :, at] * total) * inverse[
                    tile, :, at
                ]
            return carry

        lax.fori_loop(0, tiles, relax, 0, unroll=4)

    g_copies = exchange(0, grad_send)
    for count in range(3):
        sweep(count)
    g_onward = forward_on(0, g_copies)
    for count in range(3, SWEEPS - 1):
        sweep(count)

    last = odd if SWEEPS % 2 == 0 else even

    def pack(tile, carry):
        dir_send[tile] = last[tile].astype(jnp.bfloat16)
        return carry

    lax.fori_loop(0, tiles, pack, 0)
    d_copies = exchange(1, dir_send)
    d_onward = forward_on(1, d_copies)

    def unpack(which, out):
        def one(index, carry):
            group, tile = index // tiles, lax.rem(index, tiles)
            out[index] = gathered[which, group, tile].astype(jnp.float32)
            return carry

        lax.fori_loop(0, groups * tiles, one, 0)

    for copy in g_onward:
        copy.wait_recv()
    unpack(0, grad_out)
    for copy in d_onward:
        copy.wait_recv()
    unpack(1, dir_out)
    for copy in list(a_copies.values()) + p_copies + b_copies + g_copies + d_copies + g_onward + d_onward:
        copy.wait_send()


def field_stage(part, param, coef, neighbours):
    groups, tiles = lax.axis_size("sens"), lax.axis_size("par")
    rows, cells = part.shape[1:]
    f32, bf16 = jnp.float32, jnp.bfloat16
    full = jax.ShapeDtypeStruct(param.shape, f32)
    dma = pltpu.SemaphoreType.DMA
    block = (tiles, rows, cells)
    vmem, smem = pl.BlockSpec(memory_space=pltpu.VMEM), pl.BlockSpec(memory_space=pltpu.SMEM)
    sems = [(groups - 1, tiles), (tiles - 1,), (tiles - 1,), (tiles - 1,), (2, tiles - 1), (2, groups - 1, tiles)]
    return pl.pallas_call(
        functools.partial(field_kernel, groups, tiles),
        out_shape=(full, full),
        in_specs=[vmem, vmem, vmem, smem],
        out_specs=(vmem, vmem),
        scratch_shapes=[
            pltpu.VMEM((groups - 1,) + block, bf16),
            pltpu.VMEM((tiles - 1, rows, cells), f32),
            pltpu.VMEM(block, f32),
            pltpu.VMEM(block, f32),
            pltpu.VMEM((tiles, 2, cells), f32),
            pltpu.VMEM(block, f32),
            pltpu.VMEM(block, f32),
            pltpu.VMEM(block, f32),
            pltpu.VMEM(block, f32),
            pltpu.VMEM(block, f32),
            pltpu.VMEM(block, bf16),
            pltpu.VMEM(block, bf16),
            pltpu.VMEM((2, groups) + block, bf16),
        ]
        + [dma(shape) for shape in sems for _ in range(2)],
        compiler_params=pltpu.CompilerParams(collective_id=1, has_side_effects=True),
    )(part, param, coef, neighbours)


LAST = (((1,), (1,)), ((), ()))
PLAIN = (((1,), (0,)), ((), ()))


def split(values):
    high = values.astype(jnp.bfloat16)
    return high, (values - high.astype(jnp.float32)).astype(jnp.bfloat16)


def halves(table):
    high = table.astype(np.float32).astype(jnp.bfloat16)
    low = (table - high.astype(np.float64)).astype(np.float32).astype(jnp.bfloat16)
    return np.stack([high, low], 1)


def dot3(left, right, dims=PLAIN):
    parts = [(left[0], right[0]), (left[0], right[1]), (left[1], right[0])]
    high, *low = [
        lax.dot_general(a, b, dims, preferred_element_type=jnp.float32) for a, b in parts
    ]
    return high + (low[0] + low[1])


def block_tables(length, samples):
    forward, backward = tables(length)
    count = length + 1
    size = max(d for d in range(1, 65) if count % d == 0)
    padded = -(-size // 4) * 4
    blocks = count // size
    eye = np.eye(samples)

    def arrange(table):
        table = table.reshape(2, blocks, size, length)
        return np.pad(table, ((0, 0), (0, 0), (0, padded - size), (0, 0)))

    fore, back = arrange(forward), arrange(backward)
    turned = np.stack([back[1], -back[0]], 0)
    rows = samples * 2 * padded
    fields = np.einsum("jkft,bd->kbjftd", fore, eye).reshape(blocks, rows, -1)
    sensors = [
        np.einsum("jkft,bd->kbjfdt", table, eye).reshape(blocks, rows, -1)
        for table in (back, turned)
    ]
    return (
        halves(fields),
        halves(fields.transpose(0, 2, 1)),
        np.stack([halves(table) for table in sensors], 1),
        size,
        padded,
    )


def predict_kernel(padded, kernel, param, fields, sensors, series, high, low):
    size, sensor_count, cells = kernel.shape[1:]

    @pl.when(pl.program_id(0) == 0)
    def _():
        series[...] = jnp.zeros_like(series)
        first, second = split(param[...].reshape(high.shape))
        high[...] = first
        low[...] = second

    spectrum = dot3((fields[0, 0], fields[0, 1]), (high[...], low[...])).astype(jnp.bfloat16)
    columns = spectrum.shape[0]
    other = lax.rem(lax.broadcasted_iota(jnp.int32, (1, 1, columns), 2), padded)
    own = lax.broadcasted_iota(jnp.int32, (size, 1, columns), 0)
    keep = own == other
    total = jnp.zeros(series.shape, jnp.float32)
    for i in range(2):
        product = lax.dot_general(
            kernel[i].reshape(size * sensor_count, cells),
            spectrum,
            LAST,
            preferred_element_type=jnp.float32,
        ).reshape(size, sensor_count, columns)
        picked = jnp.sum(jnp.where(keep, product, 0.0), 0)
        total = total + dot3(split(picked), (sensors[0, i, 0], sensors[0, i, 1]))
    series[...] += total


def predict(kernel, param, fields, sensors, size, padded):
    blocks, _, rows, width = fields.shape
    sensor_count, cells = kernel.shape[2:]
    return pl.pallas_call(
        functools.partial(predict_kernel, padded),
        out_shape=jax.ShapeDtypeStruct((sensor_count, width), jnp.float32),
        grid=(blocks,),
        in_specs=[
            pl.BlockSpec((2, size, sensor_count, cells), lambda k: (0, k, 0, 0)),
            pl.BlockSpec(param.shape, lambda k: (0, 0, 0)),
            pl.BlockSpec((1, 2, rows, width), lambda k: (k, 0, 0, 0)),
            pl.BlockSpec((1, 2, 2, rows, width), lambda k: (k, 0, 0, 0, 0)),
        ],
        out_specs=pl.BlockSpec((sensor_count, width), lambda k: (0, 0)),
        scratch_shapes=[pltpu.VMEM((width, cells), jnp.bfloat16)] * 2,
    )(kernel, param, fields, sensors)


def backward_kernel(padded, blocks, kernel, weighted, fields, sensors, part, total):
    size, sensor_count, cells = kernel.shape[1:]
    rows = sensors.shape[3]
    pairs = size * sensor_count
    copies = lax.rem(lax.broadcasted_iota(jnp.int32, (1, pairs), 1), sensor_count)
    copies = copies == lax.broadcasted_iota(jnp.int32, (sensor_count, pairs), 0)
    copies = jnp.where(copies, 1.0, 0.0).astype(jnp.bfloat16)
    column = lax.broadcasted_iota(jnp.int32, (1, pairs), 1) // sensor_count
    keep = column == lax.rem(lax.broadcasted_iota(jnp.int32, (rows, 1), 0), padded)
    source = split(weighted[...])
    back = jnp.zeros((rows, cells), jnp.float32)
    for i in range(2):
        adjoint = dot3((sensors[0, i, 0], sensors[0, i, 1]), source, LAST)
        wide = jnp.dot(adjoint.astype(jnp.bfloat16), copies, preferred_element_type=jnp.float32)
        wide = jnp.where(keep, wide, 0.0).astype(jnp.bfloat16)
        back = back + jnp.dot(
            wide, kernel[i].reshape(pairs, cells), preferred_element_type=jnp.float32
        )
    misfit = dot3((fields[0, 0], fields[0, 1]), split(back))

    @pl.when(pl.program_id(0) == 0)
    def _():
        total[...] = jnp.zeros_like(total)

    total[...] += misfit

    @pl.when(pl.program_id(0) == blocks - 1)
    def _():
        part[...] = total[...].reshape(part.shape).astype(part.dtype)


def back_project(kernel, weighted, fields, sensors, size, padded, shape):
    blocks, _, width, rows = fields.shape
    sensor_count, cells = kernel.shape[2:]
    return pl.pallas_call(
        functools.partial(backward_kernel, padded, blocks),
        out_shape=jax.ShapeDtypeStruct(shape, jnp.bfloat16),
        grid=(blocks,),
        in_specs=[
            pl.BlockSpec((2, size, sensor_count, cells), lambda k: (0, k, 0, 0)),
            pl.BlockSpec(weighted.shape, lambda k: (0, 0)),
            pl.BlockSpec((1, 2, width, rows), lambda k: (k, 0, 0, 0)),
            pl.BlockSpec((1, 2, 2, rows, weighted.shape[1]), lambda k: (k, 0, 0, 0, 0)),
        ],
        out_specs=pl.BlockSpec(shape, lambda k: (0, 0, 0)),
        scratch_shapes=[pltpu.VMEM((width, cells), jnp.float32)],
    )(kernel, weighted, fields, sensors)


def per_device(
    kernel, param, observed, noise_scale, robust_flags, kappa_field, coupling, neighbours
):
    length, samples, cell_count = param.shape
    fields, turned, sensors, size, padded = block_tables(length, samples)
    devices = lax.axis_size("sens") * lax.axis_size("par")
    blocks = (devices, length * samples // devices, cell_count)
    flat = param.reshape(blocks)
    series = predict(kernel, flat, fields, sensors, size, padded)
    weighted = residual(
        series,
        observed,
        noise_scale,
        robust_flags,
    )
    part = back_project(
        kernel, weighted, turned, sensors, size, padded, blocks
    )
    coef = jnp.stack([coupling, kappa_field + 4.0 * coupling], 0)
    gradient, direction = field_stage(part, flat, coef, neighbours)
    return gradient.reshape(param.shape), direction.reshape(param.shape)


def solution(mesh):
    return jax.shard_map(
        per_device,
        mesh=mesh,
        in_specs=(
            P(None, None, "sens", "par"),
            P(None, None, "par"),
            P("sens", None),
            P("sens"),
            P("sens", None),
            P("par"),
            P("par"),
            P(),
        ),
        out_specs=(P(None, None, "par"), P(None, None, "par")),
        check_vma=False,
    )
```

```python
import functools

import jax
import jax.numpy as jnp
import numpy as np
from jax import lax
from jax.experimental import pallas as pl
from jax.experimental.pallas import tpu as pltpu
from jax.sharding import PartitionSpec as P

SWEEPS = 8
TSIDE = 32
LANES = 128


huber_limit = 1.345


def tables(length):
    period = 2 * length
    frequency = np.arange(length + 1)
    phases = frequency[:, None] * np.arange(length)[None, :] % period
    angles = phases * (2.0 * np.pi / period)
    cosine, sines = np.cos(angles), np.sin(angles)
    forward = np.stack([cosine, -sines], 0)
    weight = np.where((frequency == 0) | (frequency == length), 1.0, 2.0) / period
    return forward, forward * weight[:, None]


MESH = pl.DeviceIdType.MESH


def remote(src, dst, send, recv, device):
    return pltpu.make_async_remote_copy(
        src_ref=src, dst_ref=dst, send_sem=send, recv_sem=recv, device_id=device, device_id_type=MESH
    )


def residual_kernel(tiles, series, observed, noise, flags, weighted, landed, send_sem, recv_sem):
    sens, par = lax.axis_index("sens"), lax.axis_index("par")
    barrier = pltpu.get_barrier_semaphore()
    for step in range(1, tiles):
        pl.semaphore_signal(
            barrier, inc=1, device_id=(sens, lax.rem(par + step, tiles)), device_id_type=MESH
        )
    pl.semaphore_wait(barrier, tiles - 1)
    copies = []
    for step in range(1, tiles):
        copy = remote(
            series,
            landed.at[step - 1],
            send_sem.at[step - 1],
            recv_sem.at[step - 1],
            (sens, lax.rem(par + step, tiles)),
        )
        copy.start()
        copies.append(copy)
    total = series[...]
    for step, copy in enumerate(copies):
        copy.wait_recv()
        total = total + landed[step]
    samples = series.shape[1] // observed.shape[1]

    def widen(ref):
        return jnp.concatenate([ref[...]] * samples, 1)

    deviation = widen(noise)
    scaled = (total - widen(observed)) / deviation
    robust = jnp.where(
        widen(flags) == 1, jnp.clip(scaled, -huber_limit, huber_limit), scaled
    )
    weighted[...] = robust / deviation
    for copy in copies:
        copy.wait_send()


def residual(series, observed, noise_scale, robust_flags):
    tiles = lax.axis_size("par")
    spread = jnp.broadcast_to(noise_scale[:, None], observed.shape)
    return pl.pallas_call(
        functools.partial(residual_kernel, tiles),
        out_shape=jax.ShapeDtypeStruct(series.shape, jnp.float32),
        in_specs=[pl.BlockSpec(memory_space=pltpu.VMEM)] * 4,
        out_specs=pl.BlockSpec(memory_space=pltpu.VMEM),
        scratch_shapes=[
            pltpu.VMEM((tiles - 1,) + series.shape, jnp.float32),
            pltpu.SemaphoreType.DMA((tiles - 1,)),
            pltpu.SemaphoreType.DMA((tiles - 1,)),
        ],
        compiler_params=pltpu.CompilerParams(collective_id=0, has_side_effects=True),
    )(series, observed, spread, robust_flags)


def grid_sum(load, tile, near, rows, chunks):
    lane = lax.broadcasted_iota(jnp.int32, (rows, LANES), 1)
    column = lax.rem(lane, TSIDE)
    beside = [near[tile, side] for side in range(4)]
    west, east, south, north = (jnp.maximum(index, 0) for index in beside)
    has_west, has_east, has_south, has_north = (
        jnp.minimum(index + 1, 1).astype(jnp.float32) for index in beside
    )
    own = [load(tile, j) for j in range(chunks)]
    up = [pltpu.roll(v, LANES - TSIDE, 1) for v in own]
    up.append(pltpu.roll(load(north, 0), LANES - TSIDE, 1) * has_north)
    down = [pltpu.roll(load(south, chunks - 1), TSIDE, 1) * has_south]
    down += [pltpu.roll(v, TSIDE, 1) for v in own]
    sums = []
    for j in range(chunks):
        east_rim = pltpu.roll(load(east, j), TSIDE - 1, 1) * has_east
        west_rim = pltpu.roll(load(west, j), LANES - TSIDE + 1, 1) * has_west
        east_side = jnp.where(column == TSIDE - 1, east_rim, pltpu.roll(own[j], LANES - 1, 1))
        west_side = jnp.where(column == 0, west_rim, pltpu.roll(own[j], 1, 1))
        north_side = jnp.where(lane < LANES - TSIDE, up[j], up[j + 1])
        south_side = jnp.where(lane >= TSIDE, down[j + 1], down[j])
        sums.append(east_side + west_side + north_side + south_side)
    return sums


def field_kernel(
    groups, tiles, part, param, coef, near, grad_out, dir_out,
    landed, outgoing, misfit, field, coefs, grad, link, inverse, even, odd, grad_send, dir_send,
    gathered, a_send, a_recv, p_send, p_recv, c_send, c_recv, b_send, b_recv, g_send, g_recv,
    e_send, e_recv,
):
    sens, par = lax.axis_index("sens"), lax.axis_index("par")
    rows, cells = part.shape[1:]
    chunks = cells // LANES
    group_at = [lax.rem(sens + k, groups) for k in range(groups)]
    tile_at = [lax.rem(par + q, tiles) for q in range(tiles)]
    source_at = [lax.rem(par + tiles - q, tiles) for q in range(tiles)]
    beside = [
        sens + 1 - 2 * lax.rem(sens, 2),
        sens + 2 - 4 * lax.rem(sens // 2, 2),
    ]
    targets = beside if groups == 4 else group_at[1:]

    barrier = pltpu.get_barrier_semaphore()
    for k in range(1, groups):
        pl.semaphore_signal(barrier, inc=1, device_id=(group_at[k], par), device_id_type=MESH)
    for q in range(1, tiles):
        pl.semaphore_signal(barrier, inc=1, device_id=(sens, tile_at[q]), device_id_type=MESH)
    pl.semaphore_wait(barrier, groups + tiles - 2)

    order = list(range(1, tiles)) + [0]
    a_copies = {}
    for q in order:
        for k in range(1, groups):
            a_copies[k, q] = remote(
                part.at[group_at[k] * tiles + tile_at[q]],
                landed.at[k - 1, q],
                a_send.at[k - 1, q],
                a_recv.at[k - 1, q],
                (group_at[k], par),
            )
            a_copies[k, q].start()
    p_copies = []
    for q in range(1, tiles):
        device = (sens, tile_at[q])
        p_copies.append(
            remote(coef, coefs.at[par], c_send.at[q - 1], c_recv.at[q - 1], device)
        )
        p_copies.append(
            remote(
                param.at[sens * tiles + tile_at[q]],
                field.at[par],
                p_send.at[q - 1],
                p_recv.at[q - 1],
                device,
            )
        )
    for copy in p_copies:
        copy.start()
    field[par] = param[sens * tiles + par]
    coefs[par] = coef[...]

    b_copies = []
    for q in order:
        total = part[sens * tiles + tile_at[q]].astype(jnp.float32)
        for k in range(1, groups):
            a_copies[k, q].wait_recv()
            total = total + landed[k - 1, q].astype(jnp.float32)
        if q == 0:
            misfit[par] = total
        else:
            outgoing[q - 1] = total
            copy = remote(
                outgoing.at[q - 1],
                misfit.at[par],
                b_send.at[q - 1],
                b_recv.at[q - 1],
                (sens, tile_at[q]),
            )
            copy.start()
            b_copies.append(copy)
    for copy in p_copies:
        copy.wait_recv()

    def spread(tile, carry):
        both = coefs[tile]
        strength, diagonal = both[0:1], both[1:2]
        link[tile] = jnp.broadcast_to(strength, (rows, cells))
        inverse[tile] = jnp.broadcast_to(1.0 / diagonal, (rows, cells))
        for j, total in enumerate(
            grid_sum(lambda i, j: field[i, :, j * LANES : (j + 1) * LANES], tile, near, rows, chunks)
        ):
            at = slice(j * LANES, (j + 1) * LANES)
            grad[tile, :, at] = diagonal[:, at] * field[tile, :, at] - strength[:, at] * total
        return carry

    lax.fori_loop(0, tiles, spread, 0)
    for copy in b_copies:
        copy.wait_recv()

    def add_misfit(tile, carry):
        total = grad[tile] + misfit[tile]
        grad[tile] = total
        grad_send[tile] = total.astype(jnp.bfloat16)
        even[tile] = total * inverse[tile]
        return carry

    lax.fori_loop(0, tiles, add_misfit, 0)

    def exchange(which, source):
        copies = []
        for q in range(1, tiles):
            copy = remote(
                source.at[tile_at[q]],
                gathered.at[which, sens, par],
                g_send.at[which, q - 1],
                g_recv.at[which, q - 1],
                (sens, tile_at[q]),
            )
            copy.start()
            copies.append(copy)
        gathered[which, sens, par] = source[par]
        return copies

    def forward_on(which, copies):
        onward = []
        for q in range(tiles):
            if q:
                copies[q - 1].wait_recv()
            piece = gathered.at[which, sens, source_at[q]]
            for k, target in enumerate(targets):
                copy = remote(
                    piece,
                    piece,
                    e_send.at[which, k, q],
                    e_recv.at[which, k, q],
                    (target, par),
                )
                copy.start()
                onward.append(copy)
        return onward

    def relay(which, onward):
        if groups != 4:
            return onward, []
        second = []
        for q in range(tiles):
            via = q % 2
            onward[2 * q + via].wait_recv()
            piece = gathered.at[which, beside[via], source_at[q]]
            copy = remote(
                piece, piece, e_send.at[which, 2, q], e_recv.at[which, 2, q], (beside[1 - via], par)
            )
            copy.start()
            second.append(copy)
        return [onward[2 * q + 1 - q % 2] for q in range(tiles)] + second, second

    def sweep(count):
        old, new = (even, odd) if count % 2 == 0 else (odd, even)

        def relax(tile, carry):
            sums = grid_sum(
                lambda i, j: old[i, :, j * LANES : (j + 1) * LANES], tile, near, rows, chunks
            )
            for j, total in enumerate(sums):
                at = slice(j * LANES, (j + 1) * LANES)
                new[tile, :, at] = (grad[tile, :, at] + link[tile, :, at] * total) * inverse[
                    tile, :, at
                ]
            return carry

        lax.fori_loop(0, tiles, relax, 0, unroll=4)

    g_copies = exchange(0, grad_send)
    sweep(0)
    g_onward = forward_on(0, g_copies)
    for count in range(1, SWEEPS - 1):
        sweep(count)
    last = odd if SWEEPS % 2 == 0 else even

    def pack(tile, carry):
        dir_send[tile] = last[tile].astype(jnp.bfloat16)
        return carry

    lax.fori_loop(0, tiles, pack, 0)
    d_copies = exchange(1, dir_send)
    g_waits, g_second = relay(0, g_onward)
    d_onward = forward_on(1, d_copies)
    d_waits, d_second = relay(1, d_onward)

    def unpack(which, out):
        def one(index, carry):
            group, tile = index // tiles, lax.rem(index, tiles)
            out[index] = gathered[which, group, tile].astype(jnp.float32)
            return carry

        lax.fori_loop(0, groups * tiles, one, 0)

    for copy in g_waits:
        copy.wait_recv()
    unpack(0, grad_out)
    for copy in d_waits:
        copy.wait_recv()
    unpack(1, dir_out)
    started = list(a_copies.values()) + p_copies + b_copies + g_copies + d_copies
    for copy in started + g_onward + d_onward + g_second + d_second:
        copy.wait_send()


def field_stage(part, param, coef, neighbours):
    groups, tiles = lax.axis_size("sens"), lax.axis_size("par")
    rows, cells = part.shape[1:]
    f32, bf16 = jnp.float32, jnp.bfloat16
    full = jax.ShapeDtypeStruct(param.shape, f32)
    dma = pltpu.SemaphoreType.DMA
    block = (tiles, rows, cells)
    vmem, smem = pl.BlockSpec(memory_space=pltpu.VMEM), pl.BlockSpec(memory_space=pltpu.SMEM)
    sems = [(groups - 1, tiles), (tiles - 1,), (tiles - 1,), (tiles - 1,), (2, tiles - 1), (2, groups - 1, tiles)]
    return pl.pallas_call(
        functools.partial(field_kernel, groups, tiles),
        out_shape=(full, full),
        in_specs=[vmem, vmem, vmem, smem],
        out_specs=(vmem, vmem),
        scratch_shapes=[
            pltpu.VMEM((groups - 1,) + block, bf16),
            pltpu.VMEM((tiles - 1, rows, cells), f32),
            pltpu.VMEM(block, f32),
            pltpu.VMEM(block, f32),
            pltpu.VMEM((tiles, 2, cells), f32),
            pltpu.VMEM(block, f32),
            pltpu.VMEM(block, f32),
            pltpu.VMEM(block, f32),
            pltpu.VMEM(block, f32),
            pltpu.VMEM(block, f32),
            pltpu.VMEM(block, bf16),
            pltpu.VMEM(block, bf16),
            pltpu.VMEM((2, groups) + block, bf16),
        ]
        + [dma(shape) for shape in sems for _ in range(2)],
        compiler_params=pltpu.CompilerParams(collective_id=1, has_side_effects=True),
    )(part, param, coef, neighbours)


LAST = (((1,), (1,)), ((), ()))
PLAIN = (((1,), (0,)), ((), ()))


def split(values):
    high = values.astype(jnp.bfloat16)
    return high, (values - high.astype(jnp.float32)).astype(jnp.bfloat16)


def halves(table):
    high = table.astype(np.float32).astype(jnp.bfloat16)
    low = (table - high.astype(np.float64)).astype(np.float32).astype(jnp.bfloat16)
    return np.stack([high, low], 1)


def dot3(left, right, dims=PLAIN):
    parts = [(left[0], right[0]), (left[0], right[1]), (left[1], right[0])]
    high, *low = [
        lax.dot_general(a, b, dims, preferred_element_type=jnp.float32) for a, b in parts
    ]
    return high + (low[0] + low[1])


def block_tables(length, samples):
    forward, backward = tables(length)
    count = length + 1
    size = max(d for d in range(1, 65) if count % d == 0)
    padded = -(-size // 4) * 4
    blocks = count // size
    eye = np.eye(samples)

    def arrange(table):
        table = table.reshape(2, blocks, size, length)
        return np.pad(table, ((0, 0), (0, 0), (0, padded - size), (0, 0)))

    fore, back = arrange(forward), arrange(backward)
    turned = np.stack([back[1], -back[0]], 0)
    rows = samples * 2 * padded
    fields = np.einsum("jkft,bd->kbjftd", fore, eye).reshape(blocks, rows, -1)
    sensors = [
        np.einsum("jkft,bd->kbjfdt", table, eye).reshape(blocks, rows, -1)
        for table in (back, turned)
    ]
    return (
        halves(fields),
        halves(fields.transpose(0, 2, 1)),
        np.stack([halves(table) for table in sensors], 1),
        size,
        padded,
    )


def predict_kernel(padded, kernel, param, fields, sensors, series, high, low):
    size, sensor_count, cells = kernel.shape[1:]

    @pl.when(pl.program_id(0) == 0)
    def _():
        series[...] = jnp.zeros_like(series)
        first, second = split(param[...].reshape(high.shape))
        high[...] = first
        low[...] = second

    spectrum = dot3((fields[0, 0], fields[0, 1]), (high[...], low[...])).astype(jnp.bfloat16)
    columns = spectrum.shape[0]
    other = lax.rem(lax.broadcasted_iota(jnp.int32, (1, 1, columns), 2), padded)
    own = lax.broadcasted_iota(jnp.int32, (size, 1, columns), 0)
    keep = own == other
    total = jnp.zeros(series.shape, jnp.float32)
    for i in range(2):
        product = lax.dot_general(
            kernel[i].reshape(size * sensor_count, cells),
            spectrum,
            LAST,
            preferred_element_type=jnp.float32,
        ).reshape(size, sensor_count, columns)
        picked = jnp.sum(jnp.where(keep, product, 0.0), 0)
        total = total + dot3(split(picked), (sensors[0, i, 0], sensors[0, i, 1]))
    series[...] += total


def predict(kernel, param, fields, sensors, size, padded):
    blocks, _, rows, width = fields.shape
    sensor_count, cells = kernel.shape[2:]
    return pl.pallas_call(
        functools.partial(predict_kernel, padded),
        out_shape=jax.ShapeDtypeStruct((sensor_count, width), jnp.float32),
        grid=(blocks,),
        in_specs=[
            pl.BlockSpec((2, size, sensor_count, cells), lambda k: (0, k, 0, 0)),
            pl.BlockSpec(param.shape, lambda k: (0, 0, 0)),
            pl.BlockSpec((1, 2, rows, width), lambda k: (k, 0, 0, 0)),
            pl.BlockSpec((1, 2, 2, rows, width), lambda k: (k, 0, 0, 0, 0)),
        ],
        out_specs=pl.BlockSpec((sensor_count, width), lambda k: (0, 0)),
        scratch_shapes=[pltpu.VMEM((width, cells), jnp.bfloat16)] * 2,
    )(kernel, param, fields, sensors)


def backward_kernel(padded, blocks, kernel, weighted, fields, sensors, part, total):
    size, sensor_count, cells = kernel.shape[1:]
    rows = sensors.shape[3]
    pairs = size * sensor_count
    copies = lax.rem(lax.broadcasted_iota(jnp.int32, (1, pairs), 1), sensor_count)
    copies = copies == lax.broadcasted_iota(jnp.int32, (sensor_count, pairs), 0)
    copies = jnp.where(copies, 1.0, 0.0).astype(jnp.bfloat16)
    column = lax.broadcasted_iota(jnp.int32, (1, pairs), 1) // sensor_count
    keep = column == lax.rem(lax.broadcasted_iota(jnp.int32, (rows, 1), 0), padded)
    source = split(weighted[...])
    back = jnp.zeros((rows, cells), jnp.float32)
    for i in range(2):
        adjoint = dot3((sensors[0, i, 0], sensors[0, i, 1]), source, LAST)
        wide = jnp.dot(adjoint.astype(jnp.bfloat16), copies, preferred_element_type=jnp.float32)
        wide = jnp.where(keep, wide, 0.0).astype(jnp.bfloat16)
        back = back + jnp.dot(
            wide, kernel[i].reshape(pairs, cells), preferred_element_type=jnp.float32
        )
    misfit = dot3((fields[0, 0], fields[0, 1]), split(back))

    @pl.when(pl.program_id(0) == 0)
    def _():
        total[...] = jnp.zeros_like(total)

    total[...] += misfit

    @pl.when(pl.program_id(0) == blocks - 1)
    def _():
        part[...] = total[...].reshape(part.shape).astype(part.dtype)


def back_project(kernel, weighted, fields, sensors, size, padded, shape):
    blocks, _, width, rows = fields.shape
    sensor_count, cells = kernel.shape[2:]
    return pl.pallas_call(
        functools.partial(backward_kernel, padded, blocks),
        out_shape=jax.ShapeDtypeStruct(shape, jnp.bfloat16),
        grid=(blocks,),
        in_specs=[
            pl.BlockSpec((2, size, sensor_count, cells), lambda k: (0, k, 0, 0)),
            pl.BlockSpec(weighted.shape, lambda k: (0, 0)),
            pl.BlockSpec((1, 2, width, rows), lambda k: (k, 0, 0, 0)),
            pl.BlockSpec((1, 2, 2, rows, weighted.shape[1]), lambda k: (k, 0, 0, 0, 0)),
        ],
        out_specs=pl.BlockSpec(shape, lambda k: (0, 0, 0)),
        scratch_shapes=[pltpu.VMEM((width, cells), jnp.float32)],
    )(kernel, weighted, fields, sensors)


def per_device(
    kernel, param, observed, noise_scale, robust_flags, kappa_field, coupling, neighbours
):
    length, samples, cell_count = param.shape
    fields, turned, sensors, size, padded = block_tables(length, samples)
    devices = lax.axis_size("sens") * lax.axis_size("par")
    blocks = (devices, length * samples // devices, cell_count)
    flat = param.reshape(blocks)
    series = predict(kernel, flat, fields, sensors, size, padded)
    weighted = residual(
        series,
        observed,
        noise_scale,
        robust_flags,
    )
    part = back_project(
        kernel, weighted, turned, sensors, size, padded, blocks
    )
    coef = jnp.stack([coupling, kappa_field + 4.0 * coupling], 0)
    gradient, direction = field_stage(part, flat, coef, neighbours)
    return gradient.reshape(param.shape), direction.reshape(param.shape)


def solution(mesh):
    return jax.shard_map(
        per_device,
        mesh=mesh,
        in_specs=(
            P(None, None, "sens", "par"),
            P(None, None, "par"),
            P("sens", None),
            P("sens"),
            P("sens", None),
            P("par"),
            P("par"),
            P(),
        ),
        out_specs=(P(None, None, "par"), P(None, None, "par")),
        check_vma=False,
    )
```

```python
import functools

import jax
import jax.numpy as jnp
import numpy as np
from jax import lax
from jax.experimental import pallas as pl
from jax.experimental.pallas import tpu as pltpu
from jax.sharding import PartitionSpec as P

SWEEPS = 8
TSIDE = 32
LANES = 128


huber_limit = 1.345


def tables(length):
    period = 2 * length
    frequency = np.arange(length + 1)
    phases = frequency[:, None] * np.arange(length)[None, :] % period
    angles = phases * (2.0 * np.pi / period)
    cosine, sines = np.cos(angles), np.sin(angles)
    forward = np.stack([cosine, -sines], 0)
    weight = np.where((frequency == 0) | (frequency == length), 1.0, 2.0) / period
    return forward, forward * weight[:, None]


MESH = pl.DeviceIdType.MESH


def remote(src, dst, send, recv, device):
    return pltpu.make_async_remote_copy(
        src_ref=src, dst_ref=dst, send_sem=send, recv_sem=recv, device_id=device, device_id_type=MESH
    )


def residual_kernel(tiles, series, observed, noise, flags, weighted, landed, send_sem, recv_sem):
    sens, par = lax.axis_index("sens"), lax.axis_index("par")
    barrier = pltpu.get_barrier_semaphore()
    for step in range(1, tiles):
        pl.semaphore_signal(
            barrier, inc=1, device_id=(sens, lax.rem(par + step, tiles)), device_id_type=MESH
        )
    pl.semaphore_wait(barrier, tiles - 1)
    copies = []
    for step in range(1, tiles):
        copy = remote(
            series,
            landed.at[step - 1],
            send_sem.at[step - 1],
            recv_sem.at[step - 1],
            (sens, lax.rem(par + step, tiles)),
        )
        copy.start()
        copies.append(copy)
    total = series[...]
    for step, copy in enumerate(copies):
        copy.wait_recv()
        total = total + landed[step]
    samples = series.shape[1] // observed.shape[1]

    def widen(ref):
        return jnp.concatenate([ref[...]] * samples, 1)

    count = noise.shape[1]
    across = lax.broadcasted_iota(jnp.int32, (count, count), 1)
    down = lax.broadcasted_iota(jnp.int32, (count, count), 0)
    spread = jnp.where(across == down, jnp.broadcast_to(noise[...], (count, count)), 0.0)
    deviation = jnp.sum(spread, 1, keepdims=True)
    scaled = (total - widen(observed)) / deviation
    robust = jnp.where(
        widen(flags) == 1, jnp.clip(scaled, -huber_limit, huber_limit), scaled
    )
    weighted[...] = robust / deviation
    for copy in copies:
        copy.wait_send()


def residual(series, observed, noise_scale, robust_flags):
    tiles = lax.axis_size("par")
    return pl.pallas_call(
        functools.partial(residual_kernel, tiles),
        out_shape=jax.ShapeDtypeStruct(series.shape, jnp.float32),
        in_specs=[pl.BlockSpec(memory_space=pltpu.VMEM)] * 4,
        out_specs=pl.BlockSpec(memory_space=pltpu.VMEM),
        scratch_shapes=[
            pltpu.VMEM((tiles - 1,) + series.shape, jnp.float32),
            pltpu.SemaphoreType.DMA((tiles - 1,)),
            pltpu.SemaphoreType.DMA((tiles - 1,)),
        ],
        compiler_params=pltpu.CompilerParams(collective_id=0, has_side_effects=True),
    )(series, observed, noise_scale[None], robust_flags)


def grid_sum(load, tile, near, rows, chunks):
    lane = lax.broadcasted_iota(jnp.int32, (rows, LANES), 1)
    column = lax.rem(lane, TSIDE)
    beside = [near[side, tile] for side in range(4)]
    west, east, south, north = (jnp.maximum(index, 0) for index in beside)
    has_west, has_east, has_south, has_north = (
        jnp.minimum(index + 1, 1).astype(jnp.float32) for index in beside
    )
    own = [load(tile, j) for j in range(chunks)]
    up = [pltpu.roll(v, LANES - TSIDE, 1) for v in own]
    up.append(pltpu.roll(load(north, 0), LANES - TSIDE, 1) * has_north)
    down = [pltpu.roll(load(south, chunks - 1), TSIDE, 1) * has_south]
    down += [pltpu.roll(v, TSIDE, 1) for v in own]
    sums = []
    for j in range(chunks):
        east_rim = pltpu.roll(load(east, j), TSIDE - 1, 1) * has_east
        west_rim = pltpu.roll(load(west, j), LANES - TSIDE + 1, 1) * has_west
        east_side = jnp.where(column == TSIDE - 1, east_rim, pltpu.roll(own[j], LANES - 1, 1))
        west_side = jnp.where(column == 0, west_rim, pltpu.roll(own[j], 1, 1))
        north_side = jnp.where(lane < LANES - TSIDE, up[j], up[j + 1])
        south_side = jnp.where(lane >= TSIDE, down[j + 1], down[j])
        sums.append(east_side + west_side + north_side + south_side)
    return sums


def field_kernel(
    groups, tiles, part, param, kappa, coupling, near, grad_out, dir_out,
    landed, outgoing, misfit, field, kappas, couplings, grad, link, inverse, even, odd, grad_send, dir_send,
    gathered, a_send, a_recv, p_send, p_recv, c_send, c_recv, b_send, b_recv, g_send, g_recv,
    e_send, e_recv,
):
    sens, par = lax.axis_index("sens"), lax.axis_index("par")
    rows, cells = part.shape[1:]
    chunks = cells // LANES
    group_at = [lax.rem(sens + k, groups) for k in range(groups)]
    tile_at = [lax.rem(par + q, tiles) for q in range(tiles)]
    source_at = [lax.rem(par + tiles - q, tiles) for q in range(tiles)]

    barrier = pltpu.get_barrier_semaphore()
    for k in range(1, groups):
        pl.semaphore_signal(barrier, inc=1, device_id=(group_at[k], par), device_id_type=MESH)
    for q in range(1, tiles):
        pl.semaphore_signal(barrier, inc=1, device_id=(sens, tile_at[q]), device_id_type=MESH)
    pl.semaphore_wait(barrier, groups + tiles - 2)

    order = list(range(1, tiles)) + [0]
    a_copies = {}
    for q in order:
        for k in range(1, groups):
            a_copies[k, q] = remote(
                part.at[group_at[k] * tiles + tile_at[q]],
                landed.at[k - 1, q],
                a_send.at[k - 1, q],
                a_recv.at[k - 1, q],
                (group_at[k], par),
            )
            a_copies[k, q].start()
    p_copies = []
    for q in range(1, tiles):
        device = (sens, tile_at[q])
        p_copies.append(
            remote(kappa, kappas.at[par], c_send.at[0, q - 1], c_recv.at[0, q - 1], device)
        )
        p_copies.append(
            remote(coupling, couplings.at[par], c_send.at[1, q - 1], c_recv.at[1, q - 1], device)
        )
        p_copies.append(
            remote(
                param.at[sens * tiles + tile_at[q]],
                field.at[par],
                p_send.at[q - 1],
                p_recv.at[q - 1],
                device,
            )
        )
    for copy in p_copies:
        copy.start()
    field[par] = param[sens * tiles + par]
    kappas[par] = kappa[...]
    couplings[par] = coupling[...]

    b_copies = []
    for q in order:
        total = part[sens * tiles + tile_at[q]].astype(jnp.float32)
        for k in range(1, groups):
            a_copies[k, q].wait_recv()
            total = total + landed[k - 1, q].astype(jnp.float32)
        if q == 0:
            misfit[par] = total
        else:
            outgoing[q - 1] = total
            copy = remote(
                outgoing.at[q - 1],
                misfit.at[par],
                b_send.at[q - 1],
                b_recv.at[q - 1],
                (sens, tile_at[q]),
            )
            copy.start()
            b_copies.append(copy)
    for copy in p_copies:
        copy.wait_recv()

    def spread(tile, carry):
        strength = couplings[tile]
        diagonal = kappas[tile] + 4.0 * strength
        link[tile] = jnp.broadcast_to(strength, (rows, cells))
        inverse[tile] = jnp.broadcast_to(1.0 / diagonal, (rows, cells))
        for j, total in enumerate(
            grid_sum(lambda i, j: field[i, :, j * LANES : (j + 1) * LANES], tile, near, rows, chunks)
        ):
            at = slice(j * LANES, (j + 1) * LANES)
            grad[tile, :, at] = diagonal[:, at] * field[tile, :, at] - strength[:, at] * total
        return carry

    lax.fori_loop(0, tiles, spread, 0)
    for copy in b_copies:
        copy.wait_recv()

    def add_misfit(tile, carry):
        total = grad[tile] + misfit[tile]
        grad[tile] = total
        grad_send[tile] = total.astype(jnp.bfloat16)
        even[tile] = total * inverse[tile]
        return carry

    lax.fori_loop(0, tiles, add_misfit, 0)

    def exchange(which, source):
        copies = []
        for q in range(1, tiles):
            copy = remote(
                source.at[tile_at[q]],
                gathered.at[which, sens, par],
                g_send.at[which, q - 1],
                g_recv.at[which, q - 1],
                (sens, tile_at[q]),
            )
            copy.start()
            copies.append(copy)
        gathered[which, sens, par] = source[par]
        return copies

    def forward_on(which, copies):
        onward = []
        for q in range(tiles):
            if q:
                copies[q - 1].wait_recv()
            piece = gathered.at[which, sens, source_at[q]]
            for k in range(1, groups):
                copy = remote(
                    piece,
                    piece,
                    e_send.at[which, k - 1, q],
                    e_recv.at[which, k - 1, q],
                    (group_at[k], par),
                )
                copy.start()
                onward.append(copy)
        return onward

    def sweep(count):
        old, new = (even, odd) if count % 2 == 0 else (odd, even)

        def relax(tile, carry):
            sums = grid_sum(
                lambda i, j: old[i, :, j * LANES : (j + 1) * LANES], tile, near, rows, chunks
            )
            for j, total in enumerate(sums):
                at = slice(j * LANES, (j + 1) * LANES)
                new[tile, :, at] = (grad[tile, :, at] + link[tile, :, at] * total) * inverse[
                    tile, :, at
                ]
            return carry

        lax.fori_loop(0, tiles, relax, 0, unroll=4)

    g_copies = exchange(0, grad_send)
    for count in range(3):
        sweep(count)
    g_onward = forward_on(0, g_copies)
    for count in range(3, SWEEPS - 1):
        sweep(count)

    last = odd if SWEEPS % 2 == 0 else even

    def pack(tile, carry):
        dir_send[tile] = last[tile].astype(jnp.bfloat16)
        return carry

    lax.fori_loop(0, tiles, pack, 0)
    d_copies = exchange(1, dir_send)
    d_onward = forward_on(1, d_copies)

    def unpack(which, out):
        def one(index, carry):
            group, tile = index // tiles, lax.rem(index, tiles)
            out[index] = gathered[which, group, tile].astype(jnp.float32)
            return carry

        lax.fori_loop(0, groups * tiles, one, 0)

    for copy in g_onward:
        copy.wait_recv()
    unpack(0, grad_out)
    for copy in d_onward:
        copy.wait_recv()
    unpack(1, dir_out)
    for copy in list(a_copies.values()) + p_copies + b_copies + g_copies + d_copies + g_onward + d_onward:
        copy.wait_send()


def field_stage(part, param, kappa, coupling, neighbours):
    groups, tiles = lax.axis_size("sens"), lax.axis_size("par")
    rows, cells = part.shape[1:]
    f32, bf16 = jnp.float32, jnp.bfloat16
    full = jax.ShapeDtypeStruct(param.shape, f32)
    dma = pltpu.SemaphoreType.DMA
    block = (tiles, rows, cells)
    vmem, smem = pl.BlockSpec(memory_space=pltpu.VMEM), pl.BlockSpec(memory_space=pltpu.SMEM)
    sems = [(groups - 1, tiles), (tiles - 1,), (2, tiles - 1), (tiles - 1,), (2, tiles - 1), (2, groups - 1, tiles)]
    return pl.pallas_call(
        functools.partial(field_kernel, groups, tiles),
        out_shape=(full, full),
        in_specs=[vmem, vmem, vmem, vmem, smem],
        out_specs=(vmem, vmem),
        scratch_shapes=[
            pltpu.VMEM((groups - 1,) + block, bf16),
            pltpu.VMEM((tiles - 1, rows, cells), f32),
            pltpu.VMEM(block, f32),
            pltpu.VMEM(block, f32),
            pltpu.VMEM((tiles, 1, cells), f32),
            pltpu.VMEM((tiles, 1, cells), f32),
            pltpu.VMEM(block, f32),
            pltpu.VMEM(block, f32),
            pltpu.VMEM(block, f32),
            pltpu.VMEM(block, f32),
            pltpu.VMEM(block, f32),
            pltpu.VMEM(block, bf16),
            pltpu.VMEM(block, bf16),
            pltpu.VMEM((2, groups) + block, bf16),
        ]
        + [dma(shape) for shape in sems for _ in range(2)],
        compiler_params=pltpu.CompilerParams(collective_id=1, has_side_effects=True),
    )(part, param, kappa, coupling, neighbours)


LAST = (((1,), (1,)), ((), ()))
PLAIN = (((1,), (0,)), ((), ()))


def split(values):
    high = values.astype(jnp.bfloat16)
    return high, (values - high.astype(jnp.float32)).astype(jnp.bfloat16)


def halves(table):
    high = table.astype(np.float32).astype(jnp.bfloat16)
    low = (table - high.astype(np.float64)).astype(np.float32).astype(jnp.bfloat16)
    return np.stack([high, low], 1)


def dot3(left, right, dims=PLAIN):
    parts = [(left[0], right[0]), (left[0], right[1]), (left[1], right[0])]
    high, *low = [
        lax.dot_general(a, b, dims, preferred_element_type=jnp.float32) for a, b in parts
    ]
    return high + (low[0] + low[1])


def block_tables(length, samples):
    forward, backward = tables(length)
    count = length + 1
    size = max(d for d in range(1, 65) if count % d == 0)
    padded = -(-size // 4) * 4
    blocks = count // size
    eye = np.eye(samples)

    def arrange(table):
        table = table.reshape(2, blocks, size, length)
        return np.pad(table, ((0, 0), (0, 0), (0, padded - size), (0, 0)))

    fore, back = arrange(forward), arrange(backward)
    turned = np.stack([back[1], -back[0]], 0)
    rows = samples * 2 * padded
    fields = np.einsum("jkft,bd->kbjftd", fore, eye).reshape(blocks, rows, -1)
    sensors = [
        np.einsum("jkft,bd->kbjfdt", table, eye).reshape(blocks, rows, -1)
        for table in (back, turned)
    ]
    return (
        halves(fields),
        halves(fields.transpose(0, 2, 1)),
        np.stack([halves(table) for table in sensors], 1),
        size,
        padded,
    )


def predict_kernel(padded, kernel, param, fields, sensors, series, high, low):
    size, sensor_count, cells = kernel.shape[1:]

    @pl.when(pl.program_id(0) == 0)
    def _():
        series[...] = jnp.zeros_like(series)
        first, second = split(param[...].reshape(high.shape))
        high[...] = first
        low[...] = second

    spectrum = dot3((fields[0, 0], fields[0, 1]), (high[...], low[...])).astype(jnp.bfloat16)
    columns = spectrum.shape[0]
    other = lax.rem(lax.broadcasted_iota(jnp.int32, (1, 1, columns), 2), padded)
    own = lax.broadcasted_iota(jnp.int32, (size, 1, columns), 0)
    keep = own == other
    total = jnp.zeros(series.shape, jnp.float32)
    for i in range(2):
        product = lax.dot_general(
            kernel[i].reshape(size * sensor_count, cells),
            spectrum,
            LAST,
            preferred_element_type=jnp.float32,
        ).reshape(size, sensor_count, columns)
        picked = jnp.sum(jnp.where(keep, product, 0.0), 0)
        total = total + dot3(split(picked), (sensors[0, i, 0], sensors[0, i, 1]))
    series[...] += total


def predict(kernel, param, fields, sensors, size, padded):
    blocks, _, rows, width = fields.shape
    sensor_count, cells = kernel.shape[2:]
    return pl.pallas_call(
        functools.partial(predict_kernel, padded),
        out_shape=jax.ShapeDtypeStruct((sensor_count, width), jnp.float32),
        grid=(blocks,),
        in_specs=[
            pl.BlockSpec((2, size, sensor_count, cells), lambda k: (0, k, 0, 0)),
            pl.BlockSpec(param.shape, lambda k: (0, 0, 0)),
            pl.BlockSpec((1, 2, rows, width), lambda k: (k, 0, 0, 0)),
            pl.BlockSpec((1, 2, 2, rows, width), lambda k: (k, 0, 0, 0, 0)),
        ],
        out_specs=pl.BlockSpec((sensor_count, width), lambda k: (0, 0)),
        scratch_shapes=[pltpu.VMEM((width, cells), jnp.bfloat16)] * 2,
    )(kernel, param, fields, sensors)


def backward_kernel(padded, blocks, kernel, weighted, fields, sensors, part, total):
    size, sensor_count, cells = kernel.shape[1:]
    rows = sensors.shape[3]
    pairs = size * sensor_count
    copies = lax.rem(lax.broadcasted_iota(jnp.int32, (1, pairs), 1), sensor_count)
    copies = copies == lax.broadcasted_iota(jnp.int32, (sensor_count, pairs), 0)
    copies = jnp.where(copies, 1.0, 0.0).astype(jnp.bfloat16)
    column = lax.broadcasted_iota(jnp.int32, (1, pairs), 1) // sensor_count
    keep = column == lax.rem(lax.broadcasted_iota(jnp.int32, (rows, 1), 0), padded)
    source = split(weighted[...])
    back = jnp.zeros((rows, cells), jnp.float32)
    for i in range(2):
        adjoint = dot3((sensors[0, i, 0], sensors[0, i, 1]), source, LAST)
        wide = jnp.dot(adjoint.astype(jnp.bfloat16), copies, preferred_element_type=jnp.float32)
        wide = jnp.where(keep, wide, 0.0).astype(jnp.bfloat16)
        back = back + jnp.dot(
            wide, kernel[i].reshape(pairs, cells), preferred_element_type=jnp.float32
        )
    misfit = dot3((fields[0, 0], fields[0, 1]), split(back))

    @pl.when(pl.program_id(0) == 0)
    def _():
        total[...] = jnp.zeros_like(total)

    total[...] += misfit

    @pl.when(pl.program_id(0) == blocks - 1)
    def _():
        part[...] = total[...].reshape(part.shape).astype(part.dtype)


def back_project(kernel, weighted, fields, sensors, size, padded, shape):
    blocks, _, width, rows = fields.shape
    sensor_count, cells = kernel.shape[2:]
    return pl.pallas_call(
        functools.partial(backward_kernel, padded, blocks),
        out_shape=jax.ShapeDtypeStruct(shape, jnp.bfloat16),
        grid=(blocks,),
        in_specs=[
            pl.BlockSpec((2, size, sensor_count, cells), lambda k: (0, k, 0, 0)),
            pl.BlockSpec(weighted.shape, lambda k: (0, 0)),
            pl.BlockSpec((1, 2, width, rows), lambda k: (k, 0, 0, 0)),
            pl.BlockSpec((1, 2, 2, rows, weighted.shape[1]), lambda k: (k, 0, 0, 0, 0)),
        ],
        out_specs=pl.BlockSpec(shape, lambda k: (0, 0, 0)),
        scratch_shapes=[pltpu.VMEM((width, cells), jnp.float32)],
    )(kernel, weighted, fields, sensors)


def per_device(
    kernel, param, observed, noise_scale, robust_flags, kappa_field, coupling, neighbours
):
    length, samples, cell_count = param.shape
    fields, turned, sensors, size, padded = block_tables(length, samples)
    devices = lax.axis_size("sens") * lax.axis_size("par")
    blocks = (devices, length * samples // devices, cell_count)
    flat = param.reshape(blocks)
    series = predict(kernel, flat, fields, sensors, size, padded)
    weighted = residual(
        series,
        observed,
        noise_scale,
        robust_flags,
    )
    part = back_project(
        kernel, weighted, turned, sensors, size, padded, blocks
    )
    gradient, direction = field_stage(part, flat, kappa_field[None], coupling[None], neighbours.T)
    return gradient.reshape(param.shape), direction.reshape(param.shape)


def solution(mesh):
    return jax.shard_map(
        per_device,
        mesh=mesh,
        in_specs=(
            P(None, None, "sens", "par"),
            P(None, None, "par"),
            P("sens", None),
            P("sens"),
            P("sens", None),
            P("par"),
            P("par"),
            P(),
        ),
        out_specs=(P(None, None, "par"), P(None, None, "par")),
        check_vma=False,
    )
```
